512 devices in a mesh: gx: 16 (over y, z_lo), gy: 32 (over x, z_hi, core).
Axes of the slice: x: 4, y: 4, z: 16 (z_hi: 4, z_lo: 4; z = z_hi * 4 + z_lo), core: 2. Of those that a mesh axis runs over, the one named last changes fastest.
Arguments:
- inputs: bfloat16 [128, 128, 8, 128], P('gx', 'gy'), may hold values from -6 to 6
- preact: bfloat16 [128, 128, 8, 128], P('gx', 'gy'), may hold values from -6 to 6
- cotangent: bfloat16 [128, 128, 8, 128], P('gx', 'gy'), may hold values from -6 to 6
- spectral_w: bfloat16 [32, 32, 8, 128, 128], P('gx', 'gy'), may hold values from -2 to 2
- skip_w: bfloat16 [128, 128], replicated, may hold values from -0.5 to 0.5
Outputs:
- grad_inputs: bfloat16 [128, 128, 8, 128], P('gx', 'gy')
- grad_spectral: bfloat16 [32, 32, 8, 128, 128], P('gx', 'gy')
- grad_skip: float32 [128, 128], replicated
The draws below stay inside these ranges and needn't reach their ends.
All inputs are finite; a program needn't handle non-finite values.
Results may differ from the reference program's by a relative error of at most 0.0054.
Values may be sent and summed in bfloat16 or wider, within the bound.
A program may use at most 64 MiB of HBM per device.

```python
import math
import jax
import jax.numpy as jnp
from jax import lax

C = 128
MX = 32
MY = 32
MZ = 8
NZ = 8
NX = 128
NY = 128


def shard_levels(key, extent, pieces, smallest, largest):
    level, own = 1.0, jax.random.fold_in(key, 6)
    for axis_at, shards_of in pieces:
        steps = jnp.exp(jax.random.uniform(jax.random.fold_in(own, axis_at), (shards_of,), jnp.float32, smallest / len(pieces), largest / len(pieces)))
        level = level * jnp.repeat(steps, extent[axis_at] // shards_of).reshape([-1 if axis == axis_at else 1 for axis in range(len(extent))])
    return level


def bell_draw(key, extent, deviation, reach, cuts=(), kind=jnp.bfloat16):
    drawn = deviation * jax.random.normal(key, extent, jnp.float32)
    if cuts:
        drawn = drawn * shard_levels(key, extent, cuts, -0.22, 0.18)
    return jnp.clip(drawn, -reach, reach).astype(kind)


def setup_inputs(seed: int = 0) -> dict:
    splits = jax.random.split(jax.random.key(seed), 6)
    inputs = bell_draw(splits[0], (NX, NY, NZ, C), 1.0, 6.0, ((0, 16), (1, 32)))
    preact = bell_draw(splits[1], (NX, NY, NZ, C), 1.0, 6.0, ((0, 16), (1, 32)))
    cotangent = bell_draw(splits[2], (NX, NY, NZ, C), 1.0, 6.0, ((0, 16), (1, 32)))
    spectral_w = bell_draw(splits[3], (MX, MY, MZ, C, C), (C // 16) ** -0.5, 2.0, ((0, 16), (1, 32)))
    skip_w = bell_draw(splits[4], (C, C), C ** -0.5, 0.5)
    return {"inputs": inputs, "preact": preact, "cotangent": cotangent, "spectral_w": spectral_w, "skip_w": skip_w}


highest = lax.Precision.HIGHEST

def cas_table(modes, length, offset, cells):
    index = jnp.arange(modes, dtype=jnp.int32)
    freq = jnp.where(index < modes // 2, index, length - modes + index).astype(jnp.int32)
    where_cells = (offset + jnp.arange(cells, dtype=jnp.int32)).astype(jnp.int32)
    phase = freq[:, None] * where_cells[None, :] % length
    angle = phase.astype(jnp.float32) * (2.0 * math.pi / length)
    return (jnp.cos(angle) + jnp.sin(angle)) / math.sqrt(length)

def reference(inputs, preact, cotangent, spectral_w, skip_w):
    table_x = cas_table(MX, NX, 0, NX)
    table_y = cas_table(MY, NY, 0, NY)
    table_z = cas_table(MZ, NZ, 0, NZ)
    preact_wide = preact.astype(jnp.float32)
    gelu_slope = 0.5 * (1.0 + jax.scipy.special.erf(preact_wide * (1.0 / math.sqrt(2.0)))) + preact_wide * jnp.exp(-0.5 * preact_wide * preact_wide) * (1.0 / math.sqrt(2.0 * math.pi))
    grad_pre = (cotangent.astype(jnp.float32) * gelu_slope).astype(jnp.bfloat16)

    def forward(field):
        step_one = jnp.einsum('ck,ijkh->ijch', table_z, field, precision=highest)
        step_two = jnp.einsum('bj,ijch->ibch', table_y, step_one, precision=highest)
        return jnp.einsum('ai,ibch->abch', table_x, step_two, precision=highest)
    input_modes = forward(inputs.astype(jnp.float32))
    grad_modes = forward(grad_pre.astype(jnp.float32))
    grad_spectral = jnp.einsum('abcp,abcq->abcpq', input_modes, grad_modes, precision=highest).astype(jnp.bfloat16)
    back_modes = jnp.einsum('abcq,abcpq->abcp', grad_modes, spectral_w.astype(jnp.float32), precision=highest).astype(jnp.bfloat16)
    step_one = jnp.einsum('ai,abch->ibch', table_x, back_modes.astype(jnp.float32), precision=highest)
    step_two = jnp.einsum('bj,ibch->ijch', table_y, step_one, precision=highest)
    spectral_cells = jnp.einsum('ck,ijch->ijkh', table_z, step_two, precision=highest)
    flat_grad = grad_pre.reshape(-1, C)
    skip_part = lax.dot_general(flat_grad, skip_w, (((1,), (1,)), ((), ())), preferred_element_type=jnp.float32)
    grad_inputs = (skip_part.reshape(NX, NY, NZ, C) + spectral_cells).astype(jnp.bfloat16)
    local_sum = lax.dot_general(inputs.reshape(-1, C), flat_grad, (((0,), (0,)), ((), ())), preferred_element_type=jnp.float32)
    grad_skip = local_sum / math.sqrt(NX * NY * NZ)
    return (grad_inputs, grad_spectral, grad_skip)
```

```python
import functools
import math
from types import SimpleNamespace

import jax
import jax.numpy as jnp
import numpy as np
from jax import lax
from jax.experimental import pallas as pl
from jax.experimental.pallas import tpu as pltpu
from jax.sharding import PartitionSpec as P

MESH = pl.DeviceIdType.MESH
F32, BF16 = jnp.float32, jnp.bfloat16

NY, NX, NC = 4, 4, 2


def cas(modes, length):
    index = np.arange(modes)
    freq = np.where(index < modes // 2, index, length - modes + index)
    phase = freq[:, None] * np.arange(length)[None, :] % length
    angle = phase * (2.0 * math.pi / length)
    return (np.cos(angle) + np.sin(angle)) / math.sqrt(length)


def make_tables(s):
    fx = cas(2 * s.gx, 8 * s.gx)
    fy = cas(s.gy, 4 * s.gy)
    e = np.arange(2)
    jj, ii = np.arange(4), np.arange(8)
    cy, cx, cc, cj, ci = np.meshgrid(
        np.arange(NY), np.arange(NX), np.arange(NC), jj, ii, indexing="ij"
    )
    cy, cx, cc, cj, ci = (v.reshape(-1) for v in (cy, cx, cc, cj, ci))
    half = NY // NC
    xt = np.zeros((s.zl, NC, s.zl, half * 2, s.cells))
    for zl in range(s.zl):
        cell_i = 8 * (s.zl * cy + zl) + ci
        for c in range(NC):
            for zd in range(s.zl):
                for y2 in range(half):
                    a = 2 * (s.zl * (half * c + y2) + zd) + e
                    xt[zl, c, zd, y2 * 2 : y2 * 2 + 2] = fx[a][:, cell_i]
    yt = np.zeros((s.zh, s.zh, NX * NC, s.cells))
    xs, cs = (v.reshape(-1) for v in np.meshgrid(np.arange(NX), np.arange(NC), indexing="ij"))
    for zh in range(s.zh):
        cell_j = 4 * ((s.zh * cx + zh) * NC + cc) + cj
        for zd in range(s.zh):
            b = (xs * s.zh + zd) * NC + cs
            yt[zh, zd] = fy[b][:, cell_j]
    mh, ml, me, mx, mc = (
        v.reshape(-1)
        for v in np.meshgrid(
            np.arange(s.zh), np.arange(s.zl), e, np.arange(NX), np.arange(NC), indexing="ij"
        )
    )
    at = np.zeros((s.zl, NY, NY, 8, mh.size))
    for zl in range(s.zl):
        for q in range(NY):
            a = 2 * (s.zl * q + ml) + me
            for y in range(NY):
                at[zl, q, y] = fx[a][:, 8 * (s.zl * y + zl) + ii].T
    bt = np.zeros((s.zh, NX * NC, 4, mh.size))
    b = (mx * s.zh + mh) * NC + mc
    for zh in range(s.zh):
        for k in range(NX * NC):
            bt[zh, k] = fy[b][:, 4 * ((xs[k] * s.zh + zh) * NC + cs[k]) + jj].T
    return [jnp.asarray(v, F32) for v in (xt, yt, at, bt)]


def split(v):
    high = v.astype(BF16)
    return high, (v - high.astype(F32)).astype(BF16)


def kernel(s, inp, pre, cot, w, skw, xt, yt, at, bt, gi, gs, gk, r):
    gx, gy = lax.axis_index("gx"), lax.axis_index("gy")
    y, zl = gx // s.zl, gx % s.zl
    c, zh, x = gy % NC, (gy // NC) % s.zh, gy // (NC * s.zh)
    plane = (y * NX + x) * NC + c
    z = zh * s.zl + zl
    NP, NXC, NZ, NK = NY * NX * NC, NX * NC, s.zl * s.zh, s.nk
    half = NY // NC

    def at_plane(dy, dx, dc):
        yy, xx, cc = (y + dy) % NY, (x + dx) % NX, (c + dc) % NC
        return yy, xx, cc, (yy * s.zl + zl, (xx * s.zh + zh) * NC + cc)

    def at_z(dz):
        zz = (z + dz) % NZ
        return zz, (y * s.zl + zz % s.zl, (x * s.zh + zz // s.zl) * NC + c)

    def hops(d, n):
        return min(d, n - d)

    plane_steps = sorted(
        (
            (dy, dx, dc)
            for dy in range(NY)
            for dx in range(NX)
            for dc in range(NC)
            if dy + dx + dc > 0
        ),
        key=lambda t: -(hops(t[0], NY) + hops(t[1], NX)),
    )
    z_steps = sorted(range(1, NZ), key=lambda d: -hops(d, NZ))

    def send(src, dst, name, device):
        pltpu.make_async_remote_copy(
            src_ref=src,
            dst_ref=dst,
            send_sem=r.send.at[s.phase[name]],
            recv_sem=r.recv.at[s.phase[name]],
            device_id=device,
            device_id_type=MESH,
        ).start()

    def wait(ref, count, name, sems):
        part = ref.at[pl.ds(0, count)]
        pltpu.make_async_copy(part, part, sems.at[s.phase[name]]).wait()

    loads = [
        pltpu.make_async_copy(src, dst, r.local.at[n])
        for n, (src, dst) in enumerate(
            (
                (pre, r.pre),
                (cot, r.cot),
                (inp, r.inp),
                (skw, r.skw),
                (xt.at[zl, c], r.xt),
                (yt.at[zh], r.yt),
                (at.at[zl, y], r.at),
                (bt.at[zh], r.bt),
                (w, r.w),
            )
        )
    ]
    for copy in loads:
        copy.start()

    barrier = pltpu.get_barrier_semaphore()
    for step in plane_steps:
        pl.semaphore_signal(barrier, inc=1, device_id=at_plane(*step)[3], device_id_type=MESH)
    for dz in z_steps:
        pl.semaphore_signal(barrier, inc=1, device_id=at_z(dz)[1], device_id_type=MESH)

    for n in range(3):
        loads[n].wait()
    rows = 32 * NK
    p = r.pre[...].astype(F32).reshape(rows, 128)
    slope = 0.5 * (1.0 + lax.erf(p * (1.0 / math.sqrt(2.0)))) + p * jnp.exp(-0.5 * p * p) * (
        1.0 / math.sqrt(2.0 * math.pi)
    )
    grad = (r.cot[...].astype(F32).reshape(rows, 128) * slope).astype(BF16)
    r.grad[...] = grad
    r.fields[1] = grad.astype(F32)
    r.fields[0] = r.inp[...].astype(F32).reshape(rows, 128)
    for f in range(2):
        for k in range(NK):
            for j in range(0, 4, 2):
                pair = [
                    r.fields[f, pl.ds((j + o) * NK + k, 8, stride=4 * NK), :] for o in range(2)
                ]
                r.blocks[f * NK + k, pl.ds(j * 8, 16), :] = jnp.concatenate(pair, axis=0).astype(BF16)

    pl.semaphore_wait(barrier, len(plane_steps) + len(z_steps))

    for step in plane_steps:
        yy, xx, _, device = at_plane(*step)
        send(r.blocks.at[yy * NX + xx], r.slab.at[plane], "A", device)
    r.slab[plane] = r.blocks[y * NX + x]

    local = lax.dot_general(
        r.inp[...].astype(F32).reshape(rows, 128).astype(BF16),
        r.grad[...],
        (((0,), (0,)), ((), ())),
        preferred_element_type=F32,
    )
    rk = 128 // NP
    for n in range(NP):
        r.skip_a[n] = local[n * rk : (n + 1) * rk]
    for step in plane_steps:
        yy, xx, cc, device = at_plane(*step)
        send(r.skip_a.at[(yy * NX + xx) * NC + cc], r.skip_b.at[plane], "SA", device)
    r.skip_b[plane] = r.skip_a[plane]

    loads[4].wait()
    loads[5].wait()

    @pl.loop(0, NZ)
    def _(zd):
        yv = r.yt[zd // s.zl]
        xv = r.xt[zd % s.zl]
        for y2 in range(half):
            prod = jnp.concatenate(
                [xv[y2 * 2 + e : y2 * 2 + e + 1] * yv for e in range(2)], axis=0
            )
            high, low = split(prod)
            r.th[zd, pl.ds(y2 * 2 * NXC, 2 * NXC), :] = high
            r.tl[zd, pl.ds(y2 * 2 * NXC, 2 * NXC), :] = low

    wait(r.slab, NP - 1, "A", r.recv)
    slab = r.slab[...].reshape(s.cells, 128)
    nm = NZ * half * 2 * NXC
    parts = jnp.dot(r.th[...].reshape(nm, s.cells), slab, preferred_element_type=F32) + jnp.dot(
        r.tl[...].reshape(nm, s.cells), slab, preferred_element_type=F32
    )
    r.parts[...] = parts.astype(BF16).reshape(NZ, half * 2 * NXC, 128)
    for dz in z_steps:
        zz, device = at_z(dz)
        send(r.parts.at[zz], r.sums.at[z], "B", device)
    r.sums[z] = r.parts[z]

    loads[3].wait()
    r.skip[...] = lax.dot_general(
        r.grad[...], r.skw[...], (((1,), (1,)), ((), ())), preferred_element_type=F32
    )
    wait(r.skip_b, NP - 1, "SA", r.recv)
    r.skip_c[...] = jnp.sum(r.skip_b[...], axis=0)
    for dz in z_steps:
        zz, device = at_z(dz)
        send(r.skip_c, r.skip_d.at[z], "SB", device)
    r.skip_d[z] = r.skip_c[...]
    loads[6].wait()
    loads[7].wait()

    @pl.loop(0, NP)
    def _(n):
        av = r.at[n // NXC]
        bv = r.bt[n % NXC]
        for j in range(0, 4, 2):
            high, low = split(
                jnp.concatenate([av * bv[j + o : j + o + 1] for o in range(2)], axis=0)
            )
            r.uh[n, pl.ds(j * 8, 16), :] = high
            r.ul[n, pl.ds(j * 8, 16), :] = low

    wait(r.sums, NZ - 1, "B", r.recv)
    modes = jnp.sum(r.sums[...].astype(F32), axis=0)
    for y2 in range(half):
        for e in range(2):
            for k in range(NXC):
                row = (y2 * 2 + e) * NXC + k
                r.own_a[y2 * NXC + k, e : e + 1, :] = modes[row : row + 1]
    chip = y * NX + x
    mine = y // half == c
    for y2 in range(half):
        for k in range(NXC):
            yy = half * c + y2
            xx, cc = (x + k // NC) % NX, (c + k % NC) % NC
            device = (yy * s.zl + zl, (xx * s.zh + zh) * NC + cc)

            def go(yy=yy, xx=xx, cc=cc, device=device, y2=y2):
                send(r.own_a.at[y2 * NXC + xx * NC + cc], r.own_b.at[chip], "C", device)

            if k == 0:
                pl.when(yy != y)(go)
            else:
                go()

    @pl.when(mine)
    def _():
        r.own_b[chip] = r.own_a[(y % half) * NXC + x * NC + c]
        wait(r.own_b, NY * NX - 1, "C", r.recv)
        wait(r.own_a, half * NXC - 1, "C", r.send)

    @pl.when(jnp.logical_not(mine))
    def _():
        wait(r.own_b, NY * NX, "C", r.recv)
        wait(r.own_a, half * NXC, "C", r.send)

    for f in range(2):
        vals = [r.own_b[f * NK + k] for k in range(NK)]
        for m in range(NK):
            total = vals[0] * s.fz[m][0]
            for k in range(1, NK):
                total += vals[k] * s.fz[m][k]
            r.modes[f, 2 * m : 2 * m + 2, :] = total
    loads[8].wait()
    gm = r.modes[1]
    high, low = split(gm)
    lhs = jnp.concatenate([high, low], axis=0)
    nr = 2 * NK
    for m in range(NK):
        for e in range(2):
            d = lax.dot_general(
                lhs, r.w[e, 0, m], (((1,), (1,)), ((), ())), preferred_element_type=F32
            )
            row = 2 * m + e
            back = d[row : row + 1] + d[nr + row : nr + row + 1]
            r.back_a[m, e : e + 1, :] = back.astype(BF16).astype(F32)

    xc = x * NC + c
    for dy, dx, dc in plane_steps:
        if dy:
            continue
        xx, cc = (x + dx) % NX, (c + dc) % NC
        device = (gx, (xx * s.zh + zh) * NC + cc)
        send(r.back_a.at[xx * NC + cc], r.back_b.at[xc], "D", device)
    r.back_b[xc] = r.back_a[xc]

    im = jnp.transpose(r.modes[0], (1, 0))

    def outer(lo, hi):
        for row in range(lo, hi):
            r.gs[row % 2, 0, row // 2] = (im[:, row : row + 1] * gm[row : row + 1]).astype(BF16)

    outer(0, nr // 2)

    wait(r.back_b, NXC - 1, "D", r.recv)
    block = jnp.concatenate([r.back_b[:, e, :] for e in range(2)], axis=0).astype(BF16)
    r.gather_a[...] = block
    r.gather_b[z] = block
    for dz in z_steps:
        zz, device = at_z(dz)
        send(r.gather_a, r.gather_b.at[z], "E", device)
    outer(nr // 2, nr)
    out = pltpu.make_async_copy(r.gs, gs, r.local.at[9])
    out.start()

    wait(r.skip_d, NZ - 1, "SB", r.recv)
    r.skip_e[...] = jnp.sum(r.skip_d[...], axis=0) * s.scale
    for step in plane_steps:
        device = at_plane(*step)[3]
        send(r.skip_e, r.skip_f.at[plane], "SC", device)
    r.skip_f[plane] = r.skip_e[...]

    wait(r.gather_b, NZ - 1, "E", r.recv)
    gathered = r.gather_b[...].reshape(NZ * 2 * NXC, 128)
    cells = jnp.dot(
        r.uh[...].reshape(s.cells, NZ * 2 * NXC), gathered, preferred_element_type=F32
    ) + jnp.dot(r.ul[...].reshape(s.cells, NZ * 2 * NXC), gathered, preferred_element_type=F32)
    r.cells_a[...] = cells.astype(BF16).reshape(NP, 32, 128)
    for step in plane_steps:
        yy, xx, cc, device = at_plane(*step)
        send(r.cells_a.at[(yy * NX + xx) * NC + cc], r.cells_b.at[plane], "F", device)
    r.cells_b[plane] = r.cells_a[plane]

    wait(r.skip_f, NP - 1, "SC", r.recv)
    gk[...] = r.skip_f[...]

    wait(r.cells_b, NP - 1, "F", r.recv)
    vals = []
    for m in range(NK):
        total = r.cells_b[m].astype(F32)
        for q in range(1, NY):
            total += r.cells_b[q * NXC + m].astype(F32)
        vals.append(total)
    for k in range(NK):
        total = vals[0] * s.fz[0][k]
        for m in range(1, NK):
            total += vals[m] * s.fz[m][k]
        for j in range(4):
            r.fields[0, pl.ds(j * NK + k, 8, stride=4 * NK), :] = total[j * 8 : j * 8 + 8]
    gi[...] = (r.fields[0] + r.skip[...]).astype(BF16).reshape(gi.shape)

    for ref, count, name in (
        (r.slab, NP - 1, "A"),
        (r.skip_a, NP - 1, "SA"),
        (r.sums, NZ - 1, "B"),
        (r.skip_d, NZ - 1, "SB"),
        (r.back_b, NXC - 1, "D"),
        (r.gather_b, NZ - 1, "E"),
        (r.skip_f, NP - 1, "SC"),
        (r.cells_b, NP - 1, "F"),
    ):
        wait(ref, count, name, r.send)
    out.wait()


def solution(mesh):
    def on_device(inputs, preact, cotangent, spectral_w, skip_w):
        nk = inputs.shape[2]
        gx, gy = mesh.shape["gx"], mesh.shape["gy"]
        zl, zh = gx // NY, gy // (NX * NC)
        nz, np_, half, nxc = zl * zh, NY * NX * NC, NY // NC, NX * NC
        names = ("A", "SA", "B", "SB", "C", "D", "E", "SC", "F")
        table = cas(nk, nk)
        s = SimpleNamespace(
            gx=gx,
            gy=gy,
            zl=zl,
            zh=zh,
            nk=nk,
            cells=np_ * 32,
            fz=[[float(v) for v in row] for row in table],
            scale=1.0 / math.sqrt(gx * 8 * gy * 4 * nk),
            phase={name: n for n, name in enumerate(names)},
        )
        tables = make_tables(s)
        rk = 128 // np_
        V = pltpu.VMEM
        scratch = dict(
            inp=V(inputs.shape, BF16),
            pre=V(inputs.shape, BF16),
            cot=V(inputs.shape, BF16),
            skw=V((128, 128), BF16),
            w=V(spectral_w.shape, BF16),
            gs=V(spectral_w.shape, BF16),
            xt=V(tables[0].shape[2:], F32),
            yt=V(tables[1].shape[1:], F32),
            at=V(tables[2].shape[2:], F32),
            bt=V(tables[3].shape[1:], F32),
            fields=V((2, 32 * nk, 128), F32),
            grad=V((32 * nk, 128), BF16),
            skip=V((32 * nk, 128), F32),
            blocks=V((2 * nk, 32, 128), BF16),
            slab=V((np_, 32, 128), BF16),
            th=V((nz, half * 2 * nxc, s.cells), BF16),
            tl=V((nz, half * 2 * nxc, s.cells), BF16),
            parts=V((nz, half * 2 * nxc, 128), BF16),
            sums=V((nz, half * 2 * nxc, 128), BF16),
            own_a=V((half * nxc, 2, 128), F32),
            own_b=V((NY * NX, 2, 128), F32),
            modes=V((2, 2 * nk, 128), F32),
            back_a=V((nk, 2, 128), F32),
            back_b=V((nxc, 2, 128), F32),
            gather_a=V((2 * nxc, 128), BF16),
            gather_b=V((nz, 2 * nxc, 128), BF16),
            uh=V((np_, 32, nz * 2 * nxc), BF16),
            ul=V((np_, 32, nz * 2 * nxc), BF16),
            cells_a=V((np_, 32, 128), BF16),
            cells_b=V((np_, 32, 128), BF16),
            skip_a=V((np_, rk, 128), F32),
            skip_b=V((np_, rk, 128), F32),
            skip_c=V((rk, 128), F32),
            skip_d=V((nz, rk, 128), F32),
            skip_e=V((rk, 128), F32),
            skip_f=V((np_, rk, 128), F32),
            send=pltpu.SemaphoreType.DMA((len(names),)),
            recv=pltpu.SemaphoreType.DMA((len(names),)),
            local=pltpu.SemaphoreType.DMA((10,)),
        )

        def body(*refs):
            kernel(s, *refs[:12], SimpleNamespace(**dict(zip(scratch, refs[12:]))))

        any_space = pl.BlockSpec(memory_space=pl.ANY)
        vmem = pl.BlockSpec(memory_space=pltpu.VMEM)
        gi, gs, gk = pl.pallas_call(
            body,
            out_shape=(
                jax.ShapeDtypeStruct(inputs.shape, BF16),
                jax.ShapeDtypeStruct(spectral_w.shape, BF16),
                jax.ShapeDtypeStruct((np_, rk, 128), F32),
            ),
            in_specs=[any_space] * 9,
            out_specs=(vmem, any_space, vmem),
            scratch_shapes=list(scratch.values()),
            compiler_params=pltpu.CompilerParams(
                collective_id=0, has_side_effects=True, vmem_limit_bytes=32 << 20
            ),
            name="layer",
        )(inputs, preact, cotangent, spectral_w, skip_w, *tables)
        return gi, gs, gk.reshape(128, 128)

    cells = P("gx", "gy", None, None)
    weights = P("gx", "gy", None, None, None)
    return jax.shard_map(
        on_device,
        mesh=mesh,
        in_specs=(cells, cells, cells, weights, P()),
        out_specs=(cells, weights, P()),
        check_vma=False,
    )
```

```python
import functools
import math
from types import SimpleNamespace

import jax
import jax.numpy as jnp
import numpy as np
from jax import lax
from jax.experimental import pallas as pl
from jax.experimental.pallas import tpu as pltpu
from jax.sharding import PartitionSpec as P

MESH = pl.DeviceIdType.MESH
F32, BF16 = jnp.float32, jnp.bfloat16

NY, NX, NC = 4, 4, 2


def cas(modes, length):
    index = np.arange(modes)
    freq = np.where(index < modes // 2, index, length - modes + index)
    phase = freq[:, None] * np.arange(length)[None, :] % length
    angle = phase * (2.0 * math.pi / length)
    return (np.cos(angle) + np.sin(angle)) / math.sqrt(length)


def make_tables(s):
    fx = cas(2 * s.gx, 8 * s.gx)
    fy = cas(s.gy, 4 * s.gy)
    e = np.arange(2)
    jj, ii = np.arange(4), np.arange(8)
    cy, cx, cc, cj, ci = np.meshgrid(
        np.arange(NY), np.arange(NX), np.arange(NC), jj, ii, indexing="ij"
    )
    cy, cx, cc, cj, ci = (v.reshape(-1) for v in (cy, cx, cc, cj, ci))
    half = NY // NC
    xt = np.zeros((s.zl, NC, s.zl, half * 2, s.cells))
    for zl in range(s.zl):
        cell_i = 8 * (s.zl * cy + zl) + ci
        for c in range(NC):
            for zd in range(s.zl):
                for y2 in range(half):
                    a = 2 * (s.zl * (half * c + y2) + zd) + e
                    xt[zl, c, zd, y2 * 2 : y2 * 2 + 2] = fx[a][:, cell_i]
    yt = np.zeros((s.zh, s.zh, NX * NC, s.cells))
    xs, cs = (v.reshape(-1) for v in np.meshgrid(np.arange(NX), np.arange(NC), indexing="ij"))
    for zh in range(s.zh):
        cell_j = 4 * ((s.zh * cx + zh) * NC + cc) + cj
        for zd in range(s.zh):
            b = (xs * s.zh + zd) * NC + cs
            yt[zh, zd] = fy[b][:, cell_j]
    mh, ml, me, mx, mc = (
        v.reshape(-1)
        for v in np.meshgrid(
            np.arange(s.zh), np.arange(s.zl), e, np.arange(NX), np.arange(NC), indexing="ij"
        )
    )
    at = np.zeros((s.zl, NY, NY, 8, mh.size))
    for zl in range(s.zl):
        for q in range(NY):
            a = 2 * (s.zl * q + ml) + me
            for y in range(NY):
                at[zl, q, y] = fx[a][:, 8 * (s.zl * y + zl) + ii].T
    bt = np.zeros((s.zh, NX * NC, 4, mh.size))
    b = (mx * s.zh + mh) * NC + mc
    for zh in range(s.zh):
        for k in range(NX * NC):
            bt[zh, k] = fy[b][:, 4 * ((xs[k] * s.zh + zh) * NC + cs[k]) + jj].T
    return [jnp.asarray(v, F32) for v in (xt, yt, at, bt)]


def split(v):
    high = v.astype(BF16)
    return high, (v - high.astype(F32)).astype(BF16)


def kernel(s, inp, pre, cot, w, skw, xt, yt, at, bt, gi, gs, gk, r):
    gx, gy = lax.axis_index("gx"), lax.axis_index("gy")
    y, zl = gx // s.zl, gx % s.zl
    c, zh, x = gy % NC, (gy // NC) % s.zh, gy // (NC * s.zh)
    plane = (y * NX + x) * NC + c
    z = zh * s.zl + zl
    NP, NXC, NZ, NK = NY * NX * NC, NX * NC, s.zl * s.zh, s.nk
    half = NY // NC

    def at_plane(dy, dx, dc):
        yy, xx, cc = (y + dy) % NY, (x + dx) % NX, (c + dc) % NC
        return yy, xx, cc, (yy * s.zl + zl, (xx * s.zh + zh) * NC + cc)

    def at_z(dz):
        zz = (z + dz) % NZ
        return zz, (y * s.zl + zz % s.zl, (x * s.zh + zz // s.zl) * NC + c)

    def hops(d, n):
        return min(d, n - d)

    plane_steps = sorted(
        (
            (dy, dx, dc)
            for dy in range(NY)
            for dx in range(NX)
            for dc in range(NC)
            if dy + dx + dc > 0
        ),
        key=lambda t: -(hops(t[0], NY) + hops(t[1], NX)),
    )
    z_steps = sorted(range(1, NZ), key=lambda d: -hops(d, NZ))

    def send(src, dst, name, device):
        pltpu.make_async_remote_copy(
            src_ref=src,
            dst_ref=dst,
            send_sem=r.send.at[s.phase[name]],
            recv_sem=r.recv.at[s.phase[name]],
            device_id=device,
            device_id_type=MESH,
        ).start()

    def wait(ref, count, name, sems):
        part = ref.at[pl.ds(0, count)]
        pltpu.make_async_copy(part, part, sems.at[s.phase[name]]).wait()

    loads = [
        pltpu.make_async_copy(src, dst, r.local.at[n])
        for n, (src, dst) in enumerate(
            (
                (pre, r.pre),
                (cot, r.cot),
                (inp, r.inp),
                (skw, r.skw),
                (xt.at[zl, c], r.xt),
                (yt.at[zh], r.yt),
                (at.at[zl, y], r.at),
                (bt.at[zh], r.bt),
                (w, r.w),
            )
        )
    ]
    for copy in loads:
        copy.start()

    barrier = pltpu.get_barrier_semaphore()
    for step in plane_steps:
        pl.semaphore_signal(barrier, inc=1, device_id=at_plane(*step)[3], device_id_type=MESH)
    for dz in z_steps:
        pl.semaphore_signal(barrier, inc=1, device_id=at_z(dz)[1], device_id_type=MESH)

    for n in range(3):
        loads[n].wait()
    rows = 32 * NK
    p = r.pre[...].astype(F32).reshape(rows, 128)
    slope = 0.5 * (1.0 + lax.erf(p * (1.0 / math.sqrt(2.0)))) + p * jnp.exp(-0.5 * p * p) * (
        1.0 / math.sqrt(2.0 * math.pi)
    )
    grad = (r.cot[...].astype(F32).reshape(rows, 128) * slope).astype(BF16)
    r.grad[...] = grad
    r.fields[1] = grad.astype(F32)
    r.fields[0] = r.inp[...].astype(F32).reshape(rows, 128)
    for f in range(2):
        for k in range(NK):
            for j in range(0, 4, 2):
                pair = [
                    r.fields[f, pl.ds((j + o) * NK + k, 8, stride=4 * NK), :] for o in range(2)
                ]
                r.blocks[f * NK + k, pl.ds(j * 8, 16), :] = jnp.concatenate(pair, axis=0).astype(BF16)

    pl.semaphore_wait(barrier, len(plane_steps) + len(z_steps))

    for step in plane_steps:
        yy, xx, _, device = at_plane(*step)
        send(r.blocks.at[yy * NX + xx], r.slab.at[plane], "A", device)
    r.slab[plane] = r.blocks[y * NX + x]

    local = lax.dot_general(
        r.inp[...].astype(F32).reshape(rows, 128).astype(BF16),
        r.grad[...],
        (((0,), (0,)), ((), ())),
        preferred_element_type=F32,
    )
    rk = 128 // NP
    for n in range(NP):
        r.skip_a[n] = local[n * rk : (n + 1) * rk]
    loads[4].wait()
    loads[5].wait()

    @pl.loop(0, NZ)
    def _(zd):
        yv = r.yt[zd // s.zl]
        xv = r.xt[zd % s.zl]
        for y2 in range(half):
            prod = jnp.concatenate(
                [xv[y2 * 2 + e : y2 * 2 + e + 1] * yv for e in range(2)], axis=0
            )
            high, low = split(prod)
            r.th[zd, pl.ds(y2 * 2 * NXC, 2 * NXC), :] = high
            r.tl[zd, pl.ds(y2 * 2 * NXC, 2 * NXC), :] = low

    wait(r.slab, NP - 1, "A", r.recv)
    slab = r.slab[...].reshape(s.cells, 128)
    nm = NZ * half * 2 * NXC
    parts = jnp.dot(r.th[...].reshape(nm, s.cells), slab, preferred_element_type=F32) + jnp.dot(
        r.tl[...].reshape(nm, s.cells), slab, preferred_element_type=F32
    )
    r.parts[...] = parts.astype(BF16).reshape(NZ, half * 2 * NXC, 128)
    for dz in z_steps:
        zz, device = at_z(dz)
        send(r.parts.at[zz], r.sums.at[z], "B", device)
    r.sums[z] = r.parts[z]

    for step in plane_steps:
        yy, xx, cc, device = at_plane(*step)
        send(r.skip_a.at[(yy * NX + xx) * NC + cc], r.skip_b.at[plane], "SA", device)
    r.skip_b[plane] = r.skip_a[plane]
    loads[3].wait()
    r.skip[...] = lax.dot_general(
        r.grad[...], r.skw[...], (((1,), (1,)), ((), ())), preferred_element_type=F32
    )
    loads[6].wait()
    loads[7].wait()

    @pl.loop(0, NP)
    def _(n):
        av = r.at[n // NXC]
        bv = r.bt[n % NXC]
        for j in range(0, 4, 2):
            high, low = split(
                jnp.concatenate([av * bv[j + o : j + o + 1] for o in range(2)], axis=0)
            )
            r.uh[n, pl.ds(j * 8, 16), :] = high
            r.ul[n, pl.ds(j * 8, 16), :] = low

    wait(r.sums, NZ - 1, "B", r.recv)
    modes = jnp.sum(r.sums[...].astype(F32), axis=0)
    for y2 in range(half):
        for e in range(2):
            for k in range(NXC):
                row = (y2 * 2 + e) * NXC + k
                r.own_a[y2 * NXC + k, e : e + 1, :] = modes[row : row + 1]
    chip = y * NX + x
    mine = y // half == c
    for y2 in range(half):
        for k in range(NXC):
            yy = half * c + y2
            xx, cc = (x + k // NC) % NX, (c + k % NC) % NC
            device = (yy * s.zl + zl, (xx * s.zh + zh) * NC + cc)

            def go(yy=yy, xx=xx, cc=cc, device=device, y2=y2):
                send(r.own_a.at[y2 * NXC + xx * NC + cc], r.own_b.at[chip], "C", device)

            if k == 0:
                pl.when(yy != y)(go)
            else:
                go()

    wait(r.skip_b, NP - 1, "SA", r.recv)
    r.skip_c[...] = jnp.sum(r.skip_b[...], axis=0)
    for dz in z_steps:
        zz, device = at_z(dz)
        send(r.skip_c, r.skip_d.at[z], "SB", device)
    r.skip_d[z] = r.skip_c[...]

    @pl.when(mine)
    def _():
        r.own_b[chip] = r.own_a[(y % half) * NXC + x * NC + c]
        wait(r.own_b, NY * NX - 1, "C", r.recv)
        wait(r.own_a, half * NXC - 1, "C", r.send)

    @pl.when(jnp.logical_not(mine))
    def _():
        wait(r.own_b, NY * NX, "C", r.recv)
        wait(r.own_a, half * NXC, "C", r.send)

    for f in range(2):
        vals = [r.own_b[f * NK + k] for k in range(NK)]
        for m in range(NK):
            total = vals[0] * s.fz[m][0]
            for k in range(1, NK):
                total += vals[k] * s.fz[m][k]
            r.modes[f, 2 * m : 2 * m + 2, :] = total
    loads[8].wait()
    gm = r.modes[1]
    high, low = split(gm)
    lhs = jnp.concatenate([high, low], axis=0)
    nr = 2 * NK
    for m in range(NK):
        for e in range(2):
            d = lax.dot_general(
                lhs, r.w[e, 0, m], (((1,), (1,)), ((), ())), preferred_element_type=F32
            )
            row = 2 * m + e
            back = d[row : row + 1] + d[nr + row : nr + row + 1]
            r.back_a[m, e : e + 1, :] = back.astype(BF16).astype(F32)

    xc = x * NC + c
    for dy, dx, dc in plane_steps:
        if dy:
            continue
        xx, cc = (x + dx) % NX, (c + dc) % NC
        device = (gx, (xx * s.zh + zh) * NC + cc)
        send(r.back_a.at[xx * NC + cc], r.back_b.at[xc], "D", device)
    r.back_b[xc] = r.back_a[xc]

    im = jnp.transpose(r.modes[0], (1, 0))

    def outer(lo, hi):
        for row in range(lo, hi):
            r.gs[row % 2, 0, row // 2] = (im[:, row : row + 1] * gm[row : row + 1]).astype(BF16)

    outer(0, nr // 2)

    wait(r.back_b, NXC - 1, "D", r.recv)
    block = jnp.concatenate([r.back_b[:, e, :] for e in range(2)], axis=0).astype(BF16)
    r.gather_a[...] = block
    r.gather_b[z] = block
    for dz in z_steps:
        zz, device = at_z(dz)
        send(r.gather_a, r.gather_b.at[z], "E", device)
    outer(nr // 2, nr)
    out = pltpu.make_async_copy(r.gs, gs, r.local.at[9])
    out.start()

    wait(r.skip_d, NZ - 1, "SB", r.recv)
    r.skip_e[...] = jnp.sum(r.skip_d[...], axis=0) * s.scale
    for step in plane_steps:
        device = at_plane(*step)[3]
        send(r.skip_e, r.skip_f.at[plane], "SC", device)
    r.skip_f[plane] = r.skip_e[...]

    wait(r.gather_b, NZ - 1, "E", r.recv)
    gathered = r.gather_b[...].reshape(NZ * 2 * NXC, 128)
    cells = jnp.dot(
        r.uh[...].reshape(s.cells, NZ * 2 * NXC), gathered, preferred_element_type=F32
    ) + jnp.dot(r.ul[...].reshape(s.cells, NZ * 2 * NXC), gathered, preferred_element_type=F32)
    r.cells_a[...] = cells.astype(BF16).reshape(NP, 32, 128)
    for step in plane_steps:
        yy, xx, cc, device = at_plane(*step)
        send(r.cells_a.at[(yy * NX + xx) * NC + cc], r.cells_b.at[plane], "F", device)
    r.cells_b[plane] = r.cells_a[plane]

    wait(r.skip_f, NP - 1, "SC", r.recv)
    gk[...] = r.skip_f[...]

    wait(r.cells_b, NP - 1, "F", r.recv)
    vals = []
    for m in range(NK):
        total = r.cells_b[m].astype(F32)
        for q in range(1, NY):
            total += r.cells_b[q * NXC + m].astype(F32)
        vals.append(total)
    for k in range(NK):
        total = vals[0] * s.fz[0][k]
        for m in range(1, NK):
            total += vals[m] * s.fz[m][k]
        for j in range(4):
            r.fields[0, pl.ds(j * NK + k, 8, stride=4 * NK), :] = total[j * 8 : j * 8 + 8]
    gi[...] = (r.fields[0] + r.skip[...]).astype(BF16).reshape(gi.shape)

    for ref, count, name in (
        (r.slab, NP - 1, "A"),
        (r.skip_a, NP - 1, "SA"),
        (r.sums, NZ - 1, "B"),
        (r.skip_d, NZ - 1, "SB"),
        (r.back_b, NXC - 1, "D"),
        (r.gather_b, NZ - 1, "E"),
        (r.skip_f, NP - 1, "SC"),
        (r.cells_b, NP - 1, "F"),
    ):
        wait(ref, count, name, r.send)
    out.wait()


def solution(mesh):
    def on_device(inputs, preact, cotangent, spectral_w, skip_w):
        nk = inputs.shape[2]
        gx, gy = mesh.shape["gx"], mesh.shape["gy"]
        zl, zh = gx // NY, gy // (NX * NC)
        nz, np_, half, nxc = zl * zh, NY * NX * NC, NY // NC, NX * NC
        names = ("A", "SA", "B", "SB", "C", "D", "E", "SC", "F")
        table = cas(nk, nk)
        s = SimpleNamespace(
            gx=gx,
            gy=gy,
            zl=zl,
            zh=zh,
            nk=nk,
            cells=np_ * 32,
            fz=[[float(v) for v in row] for row in table],
            scale=1.0 / math.sqrt(gx * 8 * gy * 4 * nk),
            phase={name: n for n, name in enumerate(names)},
        )
        tables = make_tables(s)
        rk = 128 // np_
        V = pltpu.VMEM
        scratch = dict(
            inp=V(inputs.shape, BF16),
            pre=V(inputs.shape, BF16),
            cot=V(inputs.shape, BF16),
            skw=V((128, 128), BF16),
            w=V(spectral_w.shape, BF16),
            gs=V(spectral_w.shape, BF16),
            xt=V(tables[0].shape[2:], F32),
            yt=V(tables[1].shape[1:], F32),
            at=V(tables[2].shape[2:], F32),
            bt=V(tables[3].shape[1:], F32),
            fields=V((2, 32 * nk, 128), F32),
            grad=V((32 * nk, 128), BF16),
            skip=V((32 * nk, 128), F32),
            blocks=V((2 * nk, 32, 128), BF16),
            slab=V((np_, 32, 128), BF16),
            th=V((nz, half * 2 * nxc, s.cells), BF16),
            tl=V((nz, half * 2 * nxc, s.cells), BF16),
            parts=V((nz, half * 2 * nxc, 128), BF16),
            sums=V((nz, half * 2 * nxc, 128), BF16),
            own_a=V((half * nxc, 2, 128), F32),
            own_b=V((NY * NX, 2, 128), F32),
            modes=V((2, 2 * nk, 128), F32),
            back_a=V((nk, 2, 128), F32),
            back_b=V((nxc, 2, 128), F32),
            gather_a=V((2 * nxc, 128), BF16),
            gather_b=V((nz, 2 * nxc, 128), BF16),
            uh=V((np_, 32, nz * 2 * nxc), BF16),
            ul=V((np_, 32, nz * 2 * nxc), BF16),
            cells_a=V((np_, 32, 128), BF16),
            cells_b=V((np_, 32, 128), BF16),
            skip_a=V((np_, rk, 128), F32),
            skip_b=V((np_, rk, 128), F32),
            skip_c=V((rk, 128), F32),
            skip_d=V((nz, rk, 128), F32),
            skip_e=V((rk, 128), F32),
            skip_f=V((np_, rk, 128), F32),
            send=pltpu.SemaphoreType.DMA((len(names),)),
            recv=pltpu.SemaphoreType.DMA((len(names),)),
            local=pltpu.SemaphoreType.DMA((10,)),
        )

        def body(*refs):
            kernel(s, *refs[:12], SimpleNamespace(**dict(zip(scratch, refs[12:]))))

        any_space = pl.BlockSpec(memory_space=pl.ANY)
        vmem = pl.BlockSpec(memory_space=pltpu.VMEM)
        gi, gs, gk = pl.pallas_call(
            body,
            out_shape=(
                jax.ShapeDtypeStruct(inputs.shape, BF16),
                jax.ShapeDtypeStruct(spectral_w.shape, BF16),
                jax.ShapeDtypeStruct((np_, rk, 128), F32),
            ),
            in_specs=[any_space] * 9,
            out_specs=(vmem, any_space, vmem),
            scratch_shapes=list(scratch.values()),
            compiler_params=pltpu.CompilerParams(
                collective_id=0, has_side_effects=True
            ),
            name="layer",
        )(inputs, preact, cotangent, spectral_w, skip_w, *tables)
        return gi, gs, gk.reshape(128, 128)

    cells = P("gx", "gy", None, None)
    weights = P("gx", "gy", None, None, None)
    return jax.shard_map(
        on_device,
        mesh=mesh,
        in_specs=(cells, cells, cells, weights, P()),
        out_specs=(cells, weights, P()),
        check_vma=False,
    )
```

```python
import functools
import math
from types import SimpleNamespace

import jax
import jax.numpy as jnp
import numpy as np
from jax import lax
from jax.experimental import pallas as pl
from jax.experimental.pallas import tpu as pltpu
from jax.sharding import PartitionSpec as P

MESH = pl.DeviceIdType.MESH
F32, BF16 = jnp.float32, jnp.bfloat16

NY, NX, NC = 4, 4, 2


def cas(modes, length):
    index = np.arange(modes)
    freq = np.where(index < modes // 2, index, length - modes + index)
    phase = freq[:, None] * np.arange(length)[None, :] % length
    angle = phase * (2.0 * math.pi / length)
    return (np.cos(angle) + np.sin(angle)) / math.sqrt(length)


def make_tables(s):
    fx = cas(2 * s.gx, 8 * s.gx)
    fy = cas(s.gy, 4 * s.gy)
    e = np.arange(2)
    jj, ii = np.arange(4), np.arange(8)
    cy, cx, cc, cj, ci = np.meshgrid(
        np.arange(NY), np.arange(NX), np.arange(NC), jj, ii, indexing="ij"
    )
    cy, cx, cc, cj, ci = (v.reshape(-1) for v in (cy, cx, cc, cj, ci))
    half = NY // NC
    xt = np.zeros((s.zl, NC, s.zl, half * 2, s.cells))
    for zl in range(s.zl):
        cell_i = 8 * (s.zl * cy + zl) + ci
        for c in range(NC):
            for zd in range(s.zl):
                for y2 in range(half):
                    a = 2 * (s.zl * (half * c + y2) + zd) + e
                    xt[zl, c, zd, y2 * 2 : y2 * 2 + 2] = fx[a][:, cell_i]
    yt = np.zeros((s.zh, s.zh, NX * NC, s.cells))
    xs, cs = (v.reshape(-1) for v in np.meshgrid(np.arange(NX), np.arange(NC), indexing="ij"))
    for zh in range(s.zh):
        cell_j = 4 * ((s.zh * cx + zh) * NC + cc) + cj
        for zd in range(s.zh):
            b = (xs * s.zh + zd) * NC + cs
            yt[zh, zd] = fy[b][:, cell_j]
    mh, ml, me, mx, mc = (
        v.reshape(-1)
        for v in np.meshgrid(
            np.arange(s.zh), np.arange(s.zl), e, np.arange(NX), np.arange(NC), indexing="ij"
        )
    )
    at = np.zeros((s.zl, NY, NY, 8, mh.size))
    for zl in range(s.zl):
        for q in range(NY):
            a = 2 * (s.zl * q + ml) + me
            for y in range(NY):
                at[zl, q, y] = fx[a][:, 8 * (s.zl * y + zl) + ii].T
    bt = np.zeros((s.zh, NX * NC, 4, mh.size))
    b = (mx * s.zh + mh) * NC + mc
    for zh in range(s.zh):
        for k in range(NX * NC):
            bt[zh, k] = fy[b][:, 4 * ((xs[k] * s.zh + zh) * NC + cs[k]) + jj].T
    return [jnp.asarray(v, F32) for v in (xt, yt, at, bt)]


def split(v):
    high = v.astype(BF16)
    return high, (v - high.astype(F32)).astype(BF16)


def kernel(s, inp, pre, cot, w, skw, xt, yt, at, bt, gi, gs, gk, r):
    gx, gy = lax.axis_index("gx"), lax.axis_index("gy")
    y, zl = gx // s.zl, gx % s.zl
    c, zh, x = gy % NC, (gy // NC) % s.zh, gy // (NC * s.zh)
    plane = (y * NX + x) * NC + c
    z = zh * s.zl + zl
    NP, NXC, NZ, NK = NY * NX * NC, NX * NC, s.zl * s.zh, s.nk
    half = NY // NC

    def at_plane(dy, dx, dc):
        yy, xx, cc = (y + dy) % NY, (x + dx) % NX, (c + dc) % NC
        return yy, xx, cc, (yy * s.zl + zl, (xx * s.zh + zh) * NC + cc)

    def at_z(dz):
        zz = (z + dz) % NZ
        return zz, (y * s.zl + zz % s.zl, (x * s.zh + zz // s.zl) * NC + c)

    def hops(d, n):
        return min(d, n - d)

    plane_steps = sorted(
        (
            (dy, dx, dc)
            for dy in range(NY)
            for dx in range(NX)
            for dc in range(NC)
            if dy + dx + dc > 0
        ),
        key=lambda t: -(hops(t[0], NY) + hops(t[1], NX)),
    )
    z_steps = sorted(range(1, NZ), key=lambda d: -hops(d, NZ))

    def send(src, dst, name, device):
        pltpu.make_async_remote_copy(
            src_ref=src,
            dst_ref=dst,
            send_sem=r.send.at[s.phase[name]],
            recv_sem=r.recv.at[s.phase[name]],
            device_id=device,
            device_id_type=MESH,
        ).start()

    def wait(ref, count, name, sems):
        part = ref.at[pl.ds(0, count)]
        pltpu.make_async_copy(part, part, sems.at[s.phase[name]]).wait()

    reach = min(4, NZ // 2)
    near = [dz for dz in z_steps if hops(dz, NZ) <= reach]
    barrier = pltpu.get_barrier_semaphore()
    for step in plane_steps:
        pl.semaphore_signal(barrier, inc=1, device_id=at_plane(*step)[3], device_id_type=MESH)
    for dz in near:
        pl.semaphore_signal(barrier, inc=1, device_id=at_z(dz)[1], device_id_type=MESH)

    loads = [
        pltpu.make_async_copy(src, dst, r.local.at[n])
        for n, (src, dst) in enumerate(
            (
                (pre, r.pre),
                (cot, r.cot),
                (inp, r.inp),
                (skw, r.skw),
                (xt.at[zl, c], r.xt),
                (yt.at[zh], r.yt),
                (at.at[zl, y], r.at),
                (bt.at[zh], r.bt),
                (w, r.w),
            )
        )
    ]
    for copy in loads:
        copy.start()

    for n in range(3):
        loads[n].wait()
    rows = 32 * NK
    p = r.pre[...].astype(F32).reshape(rows, 128)
    slope = 0.5 * (1.0 + lax.erf(p * (1.0 / math.sqrt(2.0)))) + p * jnp.exp(-0.5 * p * p) * (
        1.0 / math.sqrt(2.0 * math.pi)
    )
    grad = (r.cot[...].astype(F32).reshape(rows, 128) * slope).astype(BF16)
    r.grad[...] = grad
    r.fields[1] = grad.astype(F32)
    r.fields[0] = r.inp[...].astype(F32).reshape(rows, 128)
    for f in range(2):
        for k in range(NK):
            for j in range(0, 4, 2):
                pair = [
                    r.fields[f, pl.ds((j + o) * NK + k, 8, stride=4 * NK), :] for o in range(2)
                ]
                r.blocks[f * NK + k, pl.ds(j * 8, 16), :] = jnp.concatenate(pair, axis=0).astype(BF16)

    pl.semaphore_wait(barrier, len(plane_steps) + len(near))
    relays = [dz for dz in near if hops(dz, NZ) == reach] if reach < NZ // 2 else []
    for dz in relays:
        pl.semaphore_signal(r.far, inc=1, device_id=at_z(dz)[1], device_id_type=MESH)

    for step in plane_steps:
        yy, xx, _, device = at_plane(*step)
        send(r.blocks.at[yy * NX + xx], r.slab.at[plane], "A", device)
    r.slab[plane] = r.blocks[y * NX + x]

    local = lax.dot_general(
        r.inp[...].astype(F32).reshape(rows, 128).astype(BF16),
        r.grad[...],
        (((0,), (0,)), ((), ())),
        preferred_element_type=F32,
    )
    rk = 128 // NP
    for n in range(NP):
        r.skip_a[n] = local[n * rk : (n + 1) * rk]
    loads[4].wait()
    loads[5].wait()

    order = z_steps + [0]

    def forward_table(n, dz):
        zd = (z + dz) % NZ
        yv = r.yt[zd // s.zl]
        xv = r.xt[zd % s.zl]
        for y2 in range(half):
            prod = jnp.concatenate(
                [xv[y2 * 2 + e : y2 * 2 + e + 1] * yv for e in range(2)], axis=0
            )
            high, low = split(prod)
            r.th[n, pl.ds(y2 * 2 * NXC, 2 * NXC), :] = high
            r.tl[n, pl.ds(y2 * 2 * NXC, 2 * NXC), :] = low

    for n, dz in enumerate(order):
        forward_table(n, dz)

    wait(r.slab, NP - 1, "A", r.recv)
    slab = r.slab[...].reshape(s.cells, 128)
    if relays:
        pl.semaphore_wait(r.far, len(relays))
    chunk = NZ // s.chunks
    nm = chunk * half * 2 * NXC
    for g in range(0, NZ, chunk):
        parts = jnp.dot(
            r.th[g : g + chunk].reshape(nm, s.cells), slab, preferred_element_type=F32
        ) + jnp.dot(r.tl[g : g + chunk].reshape(nm, s.cells), slab, preferred_element_type=F32)
        r.parts[g : g + chunk] = parts.astype(BF16).reshape(chunk, half * 2 * NXC, 128)
        for n in range(g, min(g + chunk, NZ - 1)):
            send(r.parts.at[n], r.sums.at[z], "B", at_z(order[n])[1])
    r.sums[z] = r.parts[NZ - 1]

    for step in plane_steps:
        yy, xx, cc, device = at_plane(*step)
        send(r.skip_a.at[(yy * NX + xx) * NC + cc], r.skip_b.at[plane], "SA", device)
    r.skip_b[plane] = r.skip_a[plane]
    loads[3].wait()
    r.skip[...] = lax.dot_general(
        r.grad[...], r.skw[...], (((1,), (1,)), ((), ())), preferred_element_type=F32
    )
    loads[6].wait()
    loads[7].wait()

    yorder = sorted(range(NY), key=lambda d: -hops(d, NY))

    @pl.loop(0, NP)
    def _(n):
        step = n // NXC
        dy = sum((jnp.where(step == g, d, 0) for g, d in enumerate(yorder)), 0)
        av = r.at[(y + dy) % NY]
        bv = r.bt[n % NXC]
        for j in range(0, 4, 2):
            high, low = split(
                jnp.concatenate([av * bv[j + o : j + o + 1] for o in range(2)], axis=0)
            )
            r.uh[n, pl.ds(j * 8, 16), :] = high
            r.ul[n, pl.ds(j * 8, 16), :] = low

    wait(r.sums, NZ - 1, "B", r.recv)
    modes = jnp.sum(r.sums[...].astype(F32), axis=0)
    for y2 in range(half):
        for e in range(2):
            for k in range(NXC):
                row = (y2 * 2 + e) * NXC + k
                r.own_a[y2 * NXC + k, e : e + 1, :] = modes[row : row + 1]
    chip = y * NX + x
    mine = y // half == c
    for y2 in range(half):
        for k in range(NXC):
            yy = half * c + y2
            xx, cc = (x + k // NC) % NX, (c + k % NC) % NC
            device = (yy * s.zl + zl, (xx * s.zh + zh) * NC + cc)

            def go(yy=yy, xx=xx, cc=cc, device=device, y2=y2):
                send(r.own_a.at[y2 * NXC + xx * NC + cc], r.own_b.at[chip], "C", device)

            if k == 0:
                pl.when(yy != y)(go)
            else:
                go()

    wait(r.skip_b, NP - 1, "SA", r.recv)
    r.skip_c[...] = jnp.sum(r.skip_b[...], axis=0)
    for dz in z_steps:
        zz, device = at_z(dz)
        send(r.skip_c, r.skip_d.at[z], "SB", device)
    r.skip_d[z] = r.skip_c[...]

    @pl.when(mine)
    def _():
        r.own_b[chip] = r.own_a[(y % half) * NXC + x * NC + c]
        wait(r.own_b, NY * NX - 1, "C", r.recv)
        wait(r.own_a, half * NXC - 1, "C", r.send)

    @pl.when(jnp.logical_not(mine))
    def _():
        wait(r.own_b, NY * NX, "C", r.recv)
        wait(r.own_a, half * NXC, "C", r.send)

    for f in range(2):
        vals = [r.own_b[f * NK + k] for k in range(NK)]
        for m in range(NK):
            total = vals[0] * s.fz[m][0]
            for k in range(1, NK):
                total += vals[k] * s.fz[m][k]
            r.modes[f, 2 * m : 2 * m + 2, :] = total
    loads[8].wait()
    gm = r.modes[1]
    high, low = split(gm)
    lhs = jnp.concatenate([high, low], axis=0)
    nr = 2 * NK
    for m in range(NK):
        for e in range(2):
            d = lax.dot_general(
                lhs, r.w[e, 0, m], (((1,), (1,)), ((), ())), preferred_element_type=F32
            )
            row = 2 * m + e
            back = d[row : row + 1] + d[nr + row : nr + row + 1]
            r.back_a[m, e : e + 1, :] = back.astype(BF16).astype(F32)

    xc = x * NC + c
    for dy, dx, dc in plane_steps:
        if dy:
            continue
        xx, cc = (x + dx) % NX, (c + dc) % NC
        device = (gx, (xx * s.zh + zh) * NC + cc)
        send(r.back_a.at[xx * NC + cc], r.back_b.at[xc], "D", device)
    r.back_b[xc] = r.back_a[xc]

    im = jnp.transpose(r.modes[0], (1, 0))

    def outer(lo, hi):
        for row in range(lo, hi):
            r.gs[row % 2, 0, row // 2] = (im[:, row : row + 1] * gm[row : row + 1]).astype(BF16)

    outer(0, nr // 2)

    wait(r.back_b, NXC - 1, "D", r.recv)
    block = jnp.concatenate([r.back_b[:, e, :] for e in range(2)], axis=0).astype(BF16)
    r.gather_a[...] = block
    r.gather_b[z] = block
    for dz in z_steps:
        zz, device = at_z(dz)
        send(r.gather_a, r.gather_b.at[z], "E", device)
    outer(nr // 2, nr)
    out = pltpu.make_async_copy(r.gs, gs, r.local.at[9])
    out.start()

    wait(r.skip_d, NZ - 1, "SB", r.recv)
    r.skip_e[...] = jnp.sum(r.skip_d[...], axis=0) * s.scale
    for step in plane_steps:
        device = at_plane(*step)[3]
        send(r.skip_e, r.skip_f.at[plane], "SC", device)
    r.skip_f[plane] = r.skip_e[...]

    wait(r.gather_b, NZ - 1, "E", r.recv)
    gathered = r.gather_b[...].reshape(NZ * 2 * NXC, 128)
    nc = NXC * 32
    for g, dy in enumerate(yorder):
        part = slice(g * NXC, (g + 1) * NXC)
        cells = jnp.dot(
            r.uh[part].reshape(nc, NZ * 2 * NXC), gathered, preferred_element_type=F32
        ) + jnp.dot(r.ul[part].reshape(nc, NZ * 2 * NXC), gathered, preferred_element_type=F32)
        r.cells_a[part] = cells.astype(BF16).reshape(NXC, 32, 128)
        for step in plane_steps:
            if step[0] == dy:
                _, xx, cc, device = at_plane(*step)
                send(r.cells_a.at[g * NXC + xx * NC + cc], r.cells_b.at[plane], "F", device)
    r.cells_b[plane] = r.cells_a[yorder.index(0) * NXC + xc]

    wait(r.skip_f, NP - 1, "SC", r.recv)
    gk[...] = r.skip_f[...]

    wait(r.cells_b, NP - 1, "F", r.recv)
    vals = []
    for m in range(NK):
        total = r.cells_b[m].astype(F32)
        for q in range(1, NY):
            total += r.cells_b[q * NXC + m].astype(F32)
        vals.append(total)
    for k in range(NK):
        total = vals[0] * s.fz[0][k]
        for m in range(1, NK):
            total += vals[m] * s.fz[m][k]
        for j in range(4):
            r.fields[0, pl.ds(j * NK + k, 8, stride=4 * NK), :] = total[j * 8 : j * 8 + 8]
    gi[...] = (r.fields[0] + r.skip[...]).astype(BF16).reshape(gi.shape)

    for ref, count, name in (
        (r.slab, NP - 1, "A"),
        (r.skip_a, NP - 1, "SA"),
        (r.sums, NZ - 1, "B"),
        (r.skip_d, NZ - 1, "SB"),
        (r.back_b, NXC - 1, "D"),
        (r.gather_b, NZ - 1, "E"),
        (r.skip_f, NP - 1, "SC"),
        (r.cells_b, NP - 1, "F"),
    ):
        wait(ref, count, name, r.send)
    out.wait()


def solution(mesh):
    def on_device(inputs, preact, cotangent, spectral_w, skip_w):
        nk = inputs.shape[2]
        gx, gy = mesh.shape["gx"], mesh.shape["gy"]
        zl, zh = gx // NY, gy // (NX * NC)
        nz, np_, half, nxc = zl * zh, NY * NX * NC, NY // NC, NX * NC
        names = ("A", "SA", "B", "SB", "C", "D", "E", "SC", "F")
        table = cas(nk, nk)
        s = SimpleNamespace(
            gx=gx,
            gy=gy,
            zl=zl,
            zh=zh,
            nk=nk,
            cells=np_ * 32,
            chunks=2,
            fz=[[float(v) for v in row] for row in table],
            scale=1.0 / math.sqrt(gx * 8 * gy * 4 * nk),
            phase={name: n for n, name in enumerate(names)},
        )
        tables = make_tables(s)
        rk = 128 // np_
        V = pltpu.VMEM
        scratch = dict(
            inp=V(inputs.shape, BF16),
            pre=V(inputs.shape, BF16),
            cot=V(inputs.shape, BF16),
            skw=V((128, 128), BF16),
            w=V(spectral_w.shape, BF16),
            gs=V(spectral_w.shape, BF16),
            xt=V(tables[0].shape[2:], F32),
            yt=V(tables[1].shape[1:], F32),
            at=V(tables[2].shape[2:], F32),
            bt=V(tables[3].shape[1:], F32),
            fields=V((2, 32 * nk, 128), F32),
            grad=V((32 * nk, 128), BF16),
            skip=V((32 * nk, 128), F32),
            blocks=V((2 * nk, 32, 128), BF16),
            slab=V((np_, 32, 128), BF16),
            th=V((nz, half * 2 * nxc, s.cells), BF16),
            tl=V((nz, half * 2 * nxc, s.cells), BF16),
            parts=V((nz, half * 2 * nxc, 128), BF16),
            sums=V((nz, half * 2 * nxc, 128), BF16),
            own_a=V((half * nxc, 2, 128), F32),
            own_b=V((NY * NX, 2, 128), F32),
            modes=V((2, 2 * nk, 128), F32),
            back_a=V((nk, 2, 128), F32),
            back_b=V((nxc, 2, 128), F32),
            gather_a=V((2 * nxc, 128), BF16),
            gather_b=V((nz, 2 * nxc, 128), BF16),
            uh=V((np_, 32, nz * 2 * nxc), BF16),
            ul=V((np_, 32, nz * 2 * nxc), BF16),
            cells_a=V((np_, 32, 128), BF16),
            cells_b=V((np_, 32, 128), BF16),
            skip_a=V((np_, rk, 128), F32),
            skip_b=V((np_, rk, 128), F32),
            skip_c=V((rk, 128), F32),
            skip_d=V((nz, rk, 128), F32),
            skip_e=V((rk, 128), F32),
            skip_f=V((np_, rk, 128), F32),
            send=pltpu.SemaphoreType.DMA((len(names),)),
            recv=pltpu.SemaphoreType.DMA((len(names),)),
            local=pltpu.SemaphoreType.DMA((10,)),
            far=pltpu.SemaphoreType.REGULAR,
        )

        def body(*refs):
            kernel(s, *refs[:12], SimpleNamespace(**dict(zip(scratch, refs[12:]))))

        any_space = pl.BlockSpec(memory_space=pl.ANY)
        vmem = pl.BlockSpec(memory_space=pltpu.VMEM)
        gi, gs, gk = pl.pallas_call(
            body,
            out_shape=(
                jax.ShapeDtypeStruct(inputs.shape, BF16),
                jax.ShapeDtypeStruct(spectral_w.shape, BF16),
                jax.ShapeDtypeStruct((np_, rk, 128), F32),
            ),
            in_specs=[pl.BlockSpec(memory_space=pltpu.HBM)] * 9,
            out_specs=(vmem, any_space, vmem),
            scratch_shapes=list(scratch.values()),
            compiler_params=pltpu.CompilerParams(
                collective_id=0, has_side_effects=True, vmem_limit_bytes=16 << 20
            ),
            name="layer",
        )(
            *(
                pltpu.with_memory_space_constraint(v, pltpu.HBM)
                for v in (inputs, preact, cotangent, spectral_w, skip_w, *tables)
            )
        )
        outs = (gi, gs, gk.reshape(128, 128))

        def store(*refs):
            copies = [pltpu.make_async_copy(refs[n], refs[3 + n], refs[6].at[n]) for n in range(3)]
            for copy in copies:
                copy.start()
            for copy in copies:
                copy.wait()

        return pl.pallas_call(
            store,
            out_shape=tuple(jax.ShapeDtypeStruct(v.shape, v.dtype) for v in outs),
            in_specs=[any_space] * 3,
            out_specs=[pl.BlockSpec(memory_space=pltpu.HBM)] * 3,
            scratch_shapes=[pltpu.SemaphoreType.DMA((3,))],
            compiler_params=pltpu.CompilerParams(vmem_limit_bytes=4 << 20),
            name="store",
        )(*outs)

    cells = P("gx", "gy", None, None)
    weights = P("gx", "gy", None, None, None)
    return jax.shard_map(
        on_device,
        mesh=mesh,
        in_specs=(cells, cells, cells, weights, P()),
        out_specs=(cells, weights, P()),
        check_vma=False,
    )
```

```python
import functools
import math
from types import SimpleNamespace

import jax
import jax.numpy as jnp
import numpy as np
from jax import lax
from jax.experimental import pallas as pl
from jax.experimental.pallas import tpu as pltpu
from jax.sharding import PartitionSpec as P

MESH = pl.DeviceIdType.MESH
F32, BF16 = jnp.float32, jnp.bfloat16

NY, NX, NC = 4, 4, 2


def cas(modes, length):
    index = np.arange(modes)
    freq = np.where(index < modes // 2, index, length - modes + index)
    phase = freq[:, None] * np.arange(length)[None, :] % length
    angle = phase * (2.0 * math.pi / length)
    return (np.cos(angle) + np.sin(angle)) / math.sqrt(length)


def make_tables(s):
    fx = cas(2 * s.gx, 8 * s.gx)
    fy = cas(s.gy, 4 * s.gy)
    e = np.arange(2)
    jj, ii = np.arange(4), np.arange(8)
    cy, cx, cc, cj, ci = np.meshgrid(
        np.arange(NY), np.arange(NX), np.arange(NC), jj, ii, indexing="ij"
    )
    cy, cx, cc, cj, ci = (v.reshape(-1) for v in (cy, cx, cc, cj, ci))
    xt = np.zeros((s.zl, NY, s.zl, 2, s.cells))
    for zl in range(s.zl):
        cell_i = 8 * (s.zl * cy + zl) + ci
        for y in range(NY):
            for zd in range(s.zl):
                xt[zl, y, zd] = fx[2 * (s.zl * y + zd) + e][:, cell_i]
    yt = np.zeros((s.zh, s.zh, 2 * NX * NC, s.cells))
    xs, cs = (v.reshape(-1) for v in np.meshgrid(np.arange(NX), np.arange(NC), indexing="ij"))
    for zh in range(s.zh):
        cell_j = 4 * ((s.zh * cx + zh) * NC + cc) + cj
        for zd in range(s.zh):
            b = (xs * s.zh + zd) * NC + cs
            yt[zh, zd] = np.repeat(fy[b][:, cell_j], 2, axis=0)
    mh, ml, mx, mc, me = (
        v.reshape(-1)
        for v in np.meshgrid(
            np.arange(s.zh), np.arange(s.zl), np.arange(NX), np.arange(NC), e, indexing="ij"
        )
    )
    at = np.zeros((s.zl, NY, NY, 8, mh.size))
    for zl in range(s.zl):
        for q in range(NY):
            a = 2 * (s.zl * q + ml) + me
            for y in range(NY):
                at[zl, q, y] = fx[a][:, 8 * (s.zl * y + zl) + ii].T
    bt = np.zeros((s.zh, NX * NC, 4, mh.size))
    b = (mx * s.zh + mh) * NC + mc
    for zh in range(s.zh):
        for k in range(NX * NC):
            bt[zh, k] = fy[b][:, 4 * ((xs[k] * s.zh + zh) * NC + cs[k]) + jj].T
    return [jnp.asarray(v, F32) for v in (xt, yt, at, bt)]


def split(v):
    high = v.astype(BF16)
    return high, (v - high.astype(F32)).astype(BF16)


def kernel(s, inp, pre, cot, w, skw, xt, yt, at, bt, gi, gs, gk, r):
    gx, gy = lax.axis_index("gx"), lax.axis_index("gy")
    y, zl = gx // s.zl, gx % s.zl
    c, zh, x = gy % NC, (gy // NC) % s.zh, gy // (NC * s.zh)
    plane = (y * NX + x) * NC + c
    z = zh * s.zl + zl
    NP, NXC, NZ, NK = NY * NX * NC, NX * NC, s.zl * s.zh, s.nk

    def at_plane(dy, dx, dc):
        yy, xx, cc = (y + dy) % NY, (x + dx) % NX, (c + dc) % NC
        return yy, xx, cc, (yy * s.zl + zl, (xx * s.zh + zh) * NC + cc)

    def at_z(dz):
        zz = (z + dz) % NZ
        return zz, (y * s.zl + zz % s.zl, (x * s.zh + zz // s.zl) * NC + c)

    def hops(d, n):
        return min(d, n - d)

    plane_steps = sorted(
        (
            (dy, dx, dc)
            for dy in range(NY)
            for dx in range(NX)
            for dc in range(NC)
            if dy + dx + dc > 0
        ),
        key=lambda t: -(hops(t[0], NY) + hops(t[1], NX)),
    )
    z_steps = sorted(range(1, NZ), key=lambda d: -hops(d, NZ))

    def send(src, dst, name, device):
        pltpu.make_async_remote_copy(
            src_ref=src,
            dst_ref=dst,
            send_sem=r.send.at[s.phase[name]],
            recv_sem=r.recv.at[s.phase[name]],
            device_id=device,
            device_id_type=MESH,
        ).start()

    def wait(ref, count, name, sems):
        part = ref.at[pl.ds(0, count)]
        pltpu.make_async_copy(part, part, sems.at[s.phase[name]]).wait()

    reach = min(4, NZ // 2)
    near = [dz for dz in z_steps if hops(dz, NZ) <= reach]
    barrier = pltpu.get_barrier_semaphore()
    for step in plane_steps:
        pl.semaphore_signal(barrier, inc=1, device_id=at_plane(*step)[3], device_id_type=MESH)
    for dz in near:
        pl.semaphore_signal(barrier, inc=1, device_id=at_z(dz)[1], device_id_type=MESH)

    loads = [
        pltpu.make_async_copy(src, dst, r.local.at[n])
        for n, (src, dst) in enumerate(
            (
                (pre, r.pre),
                (cot, r.cot),
                (inp, r.inp),
                (skw, r.skw),
                (xt.at[zl, y], r.xt),
                (yt.at[zh], r.yt),
                (at.at[zl, y], r.at),
                (bt.at[zh], r.bt),
                (w, r.w),
            )
        )
    ]
    for copy in loads:
        copy.start()

    for n in range(2):
        loads[n].wait()
    rows = 32 * NK
    p = r.pre[...].astype(F32).reshape(rows, 128)
    slope = 0.5 * (1.0 + lax.erf(p * (1.0 / math.sqrt(2.0)))) + p * jnp.exp(-0.5 * p * p) * (
        1.0 / math.sqrt(2.0 * math.pi)
    )
    grad = (r.cot[...].astype(F32).reshape(rows, 128) * slope).astype(BF16)
    r.grad[...] = grad
    r.fields[1] = grad.astype(F32)

    def make_blocks(f):
        for k in range(NK):
            for j in range(0, 4, 2):
                pair = [
                    r.fields[f, pl.ds((j + o) * NK + k, 8, stride=4 * NK), :] for o in range(2)
                ]
                r.blocks[f, k, pl.ds(j * 8, 16), :] = jnp.concatenate(pair, axis=0).astype(BF16)

    make_blocks(1)

    pl.semaphore_wait(barrier, len(plane_steps) + len(near))
    relays = [dz for dz in near if hops(dz, NZ) == reach] if reach < NZ // 2 else []
    for dz in relays:
        pl.semaphore_signal(r.far, inc=1, device_id=at_z(dz)[1], device_id_type=MESH)

    xc = x * NC + c
    slot = z * NXC + xc

    def phase_a(f):
        for step in plane_steps:
            _, xx, cc, device = at_plane(*step)
            send(r.blocks.at[f, xx * NC + cc], r.slab.at[f, plane], f"A{f}", device)
        r.slab[f, plane] = r.blocks[f, xc]

    phase_a(1)

    order = z_steps + [0]
    loads[4].wait()
    loads[5].wait()
    for n, dz in enumerate(order):
        zd = (z + dz) % NZ
        yv = r.yt[zd // s.zl]
        xv = r.xt[zd % s.zl]
        high, low = split(jnp.concatenate([xv] * NXC, axis=0) * yv)
        r.th[n] = high
        r.tl[n] = low

    loads[2].wait()
    r.fields[0] = r.inp[...].astype(F32).reshape(rows, 128)
    make_blocks(0)
    local = lax.dot_general(
        r.fields[0].astype(BF16),
        r.grad[...],
        (((0,), (0,)), ((), ())),
        preferred_element_type=F32,
    )
    rk = 128 // NP
    for n in range(NP):
        r.skip_a[n] = local[n * rk : (n + 1) * rk]

    def sheet(dzs):
        steps = [(dz, dx, dc) for dz in dzs for dx in range(NX) for dc in range(NC)]
        return sorted(
            (t for t in steps if sum(t)), key=lambda t: -(hops(t[0], NZ) + hops(t[1], NX))
        )

    def at_sheet(dz, dx, dc):
        zz, xx, cc = (z + dz) % NZ, (x + dx) % NX, (c + dc) % NC
        return xx * NC + cc, (y * s.zl + zz % s.zl, (xx * s.zh + zz // s.zl) * NC + cc)

    def phase_b(f, chunks):
        slab = r.slab[f].reshape(s.cells, 128)
        chunk = NZ // chunks
        nm = chunk * 2 * NXC
        for g in range(0, NZ, chunk):
            parts = jnp.dot(
                r.th[g : g + chunk].reshape(nm, s.cells), slab, preferred_element_type=F32
            ) + jnp.dot(r.tl[g : g + chunk].reshape(nm, s.cells), slab, preferred_element_type=F32)
            r.parts[f, g : g + chunk] = parts.astype(BF16).reshape(chunk, NXC, 2, 128)
            for step in sheet(order[g : g + chunk]):
                k, device = at_sheet(*step)
                send(r.parts.at[f, order.index(step[0]), k], r.sums.at[f, slot], f"B{f}", device)
        r.sums[f, slot] = r.parts[f, NZ - 1, xc]

    row_steps = [t for t in plane_steps if t[0] == 0]
    if relays:
        pl.semaphore_wait(r.far, len(relays))
    for step in row_steps:
        pl.semaphore_signal(r.row, inc=1, device_id=at_plane(*step)[3], device_id_type=MESH)
    wait(r.slab.at[1], NP - 1, "A1", r.recv)
    pl.semaphore_wait(r.row, len(row_steps))
    phase_b(1, s.chunks)

    phase_a(0)
    for step in plane_steps:
        yy, xx, cc, device = at_plane(*step)
        send(r.skip_a.at[(yy * NX + xx) * NC + cc], r.skip_b.at[plane], "SA", device)
    r.skip_b[plane] = r.skip_a[plane]
    loads[3].wait()
    r.skip[...] = lax.dot_general(
        r.grad[...], r.skw[...], (((1,), (1,)), ((), ())), preferred_element_type=F32
    )
    loads[6].wait()
    loads[7].wait()
    yorder = sorted(range(NY), key=lambda d: -hops(d, NY))

    @pl.loop(0, NP)
    def _(n):
        step = n // NXC
        dy = sum((jnp.where(step == g, d, 0) for g, d in enumerate(yorder)), 0)
        av = r.at[(y + dy) % NY]
        bv = r.bt[n % NXC]
        for j in range(0, 4, 2):
            high, low = split(
                jnp.concatenate([av * bv[j + o : j + o + 1] for o in range(2)], axis=0)
            )
            r.uh[n, pl.ds(j * 8, 16), :] = high
            r.ul[n, pl.ds(j * 8, 16), :] = low

    wait(r.skip_b, NP - 1, "SA", r.recv)
    r.skip_c[...] = jnp.sum(r.skip_b[...], axis=0)
    for dz in z_steps:
        device = at_z(dz)[1]
        send(r.skip_c, r.skip_d.at[z], "SB", device)
    r.skip_d[z] = r.skip_c[...]

    def owned(f):
        wait(r.sums.at[f], NZ * NXC - 1, f"B{f}", r.recv)
        total = jnp.sum(r.sums[f].reshape(NZ, 2 * NXC, 128).astype(F32), axis=0)
        r.own[...] = total
        vals = [r.own[2 * k : 2 * k + 2] for k in range(NK)]
        for m in range(NK):
            total = vals[0] * s.fz[m][0]
            for k in range(1, NK):
                total += vals[k] * s.fz[m][k]
            r.modes[f, 2 * m : 2 * m + 2, :] = total

    loads[8].wait()
    owned(1)
    gm = r.modes[1]
    high, low = split(gm)
    lhs = jnp.concatenate([high, low], axis=0)
    nr = 2 * NK
    for m in range(NK):
        for e in range(2):
            d = lax.dot_general(
                lhs, r.w[e, 0, m], (((1,), (1,)), ((), ())), preferred_element_type=F32
            )
            row = 2 * m + e
            back = d[row : row + 1] + d[nr + row : nr + row + 1]
            r.back[row : row + 1, :] = back
    r.back_a[...] = r.back[...].astype(BF16).reshape(NK, 2, 128)

    for step in sheet(order):
        k, device = at_sheet(*step)
        send(r.back_a.at[k], r.gather.at[slot], "D", device)
    r.gather[slot] = r.back_a[xc]

    wait(r.slab.at[0], NP - 1, "A0", r.recv)
    phase_b(0, 1)

    wait(r.skip_d, NZ - 1, "SB", r.recv)
    r.skip_e[...] = jnp.sum(r.skip_d[...], axis=0) * s.scale
    for step in plane_steps:
        device = at_plane(*step)[3]
        send(r.skip_e, r.skip_f.at[plane], "SC", device)
    r.skip_f[plane] = r.skip_e[...]

    wait(r.gather, NZ * NXC - 1, "D", r.recv)
    gathered = r.gather[...].reshape(NZ * 2 * NXC, 128)
    nc = NXC * 32
    for g, dy in enumerate(yorder):
        part = slice(g * NXC, (g + 1) * NXC)
        cells = jnp.dot(
            r.uh[part].reshape(nc, NZ * 2 * NXC), gathered, preferred_element_type=F32
        ) + jnp.dot(r.ul[part].reshape(nc, NZ * 2 * NXC), gathered, preferred_element_type=F32)
        r.cells_a[part] = cells.astype(BF16).reshape(NXC, 32, 128)
        for step in plane_steps:
            if step[0] == dy:
                _, xx, cc, device = at_plane(*step)
                send(r.cells_a.at[g * NXC + xx * NC + cc], r.cells_b.at[plane], "F", device)
    r.cells_b[plane] = r.cells_a[yorder.index(0) * NXC + xc]

    owned(0)
    im = jnp.transpose(r.modes[0], (1, 0))
    for row in range(nr):
        gs[row % 2, 0, row // 2] = (im[:, row : row + 1] * gm[row : row + 1]).astype(BF16)

    wait(r.skip_f, NP - 1, "SC", r.recv)
    gk[...] = r.skip_f[...]

    wait(r.cells_b, NP - 1, "F", r.recv)
    vals = []
    for m in range(NK):
        total = r.cells_b[m].astype(F32)
        for q in range(1, NY):
            total += r.cells_b[q * NXC + m].astype(F32)
        vals.append(total)
    for k in range(NK):
        total = vals[0] * s.fz[0][k]
        for m in range(1, NK):
            total += vals[m] * s.fz[m][k]
        for j in range(4):
            r.fields[0, pl.ds(j * NK + k, 8, stride=4 * NK), :] = total[j * 8 : j * 8 + 8]
    gi[...] = (r.fields[0] + r.skip[...]).astype(BF16).reshape(gi.shape)

    for ref, count, name in (
        (r.slab.at[1], NP - 1, "A1"),
        (r.slab.at[0], NP - 1, "A0"),
        (r.skip_a, NP - 1, "SA"),
        (r.sums.at[1], NZ * NXC - 1, "B1"),
        (r.sums.at[0], NZ * NXC - 1, "B0"),
        (r.skip_d, NZ - 1, "SB"),
        (r.gather, NZ * NXC - 1, "D"),
        (r.skip_f, NP - 1, "SC"),
        (r.cells_b, NP - 1, "F"),
    ):
        wait(ref, count, name, r.send)


def solution(mesh):
    def on_device(inputs, preact, cotangent, spectral_w, skip_w):
        nk = inputs.shape[2]
        gx, gy = mesh.shape["gx"], mesh.shape["gy"]
        zl, zh = gx // NY, gy // (NX * NC)
        nz, np_, nxc = zl * zh, NY * NX * NC, NX * NC
        names = ("A0", "A1", "SA", "B0", "B1", "SB", "D", "SC", "F")
        table = cas(nk, nk)
        s = SimpleNamespace(
            gx=gx,
            gy=gy,
            zl=zl,
            zh=zh,
            nk=nk,
            cells=np_ * 32,
            chunks=2,
            fz=[[float(v) for v in row] for row in table],
            scale=1.0 / math.sqrt(gx * 8 * gy * 4 * nk),
            phase={name: n for n, name in enumerate(names)},
        )
        tables = make_tables(s)
        rk = 128 // np_
        V = pltpu.VMEM
        scratch = dict(
            inp=V(inputs.shape, BF16),
            pre=V(inputs.shape, BF16),
            cot=V(inputs.shape, BF16),
            skw=V((128, 128), BF16),
            w=V(spectral_w.shape, BF16),
            xt=V(tables[0].shape[2:], F32),
            yt=V(tables[1].shape[1:], F32),
            at=V(tables[2].shape[2:], F32),
            bt=V(tables[3].shape[1:], F32),
            fields=V((2, 32 * nk, 128), F32),
            grad=V((32 * nk, 128), BF16),
            skip=V((32 * nk, 128), F32),
            blocks=V((2, nk, 32, 128), BF16),
            slab=V((2, np_, 32, 128), BF16),
            th=V((nz, 2 * nxc, s.cells), BF16),
            tl=V((nz, 2 * nxc, s.cells), BF16),
            parts=V((2, nz, nxc, 2, 128), BF16),
            sums=V((2, nz * nxc, 2, 128), BF16),
            own=V((2 * nxc, 128), F32),
            modes=V((2, 2 * nk, 128), F32),
            back=V((2 * nk, 128), F32),
            back_a=V((nk, 2, 128), BF16),
            gather=V((nz * nxc, 2, 128), BF16),
            uh=V((np_, 32, nz * 2 * nxc), BF16),
            ul=V((np_, 32, nz * 2 * nxc), BF16),
            cells_a=V((np_, 32, 128), BF16),
            cells_b=V((np_, 32, 128), BF16),
            skip_a=V((np_, rk, 128), F32),
            skip_b=V((np_, rk, 128), F32),
            skip_c=V((rk, 128), F32),
            skip_d=V((nz, rk, 128), F32),
            skip_e=V((rk, 128), F32),
            skip_f=V((np_, rk, 128), F32),
            send=pltpu.SemaphoreType.DMA((len(names),)),
            recv=pltpu.SemaphoreType.DMA((len(names),)),
            local=pltpu.SemaphoreType.DMA((9,)),
            far=pltpu.SemaphoreType.REGULAR,
            row=pltpu.SemaphoreType.REGULAR,
        )

        def body(*refs):
            kernel(s, *refs[:12], SimpleNamespace(**dict(zip(scratch, refs[12:]))))

        any_space = pl.BlockSpec(memory_space=pl.ANY)
        vmem = pl.BlockSpec(memory_space=pltpu.VMEM)
        gi, gs, gk = pl.pallas_call(
            body,
            out_shape=(
                jax.ShapeDtypeStruct(inputs.shape, BF16),
                jax.ShapeDtypeStruct(spectral_w.shape, BF16),
                jax.ShapeDtypeStruct((np_, rk, 128), F32),
            ),
            in_specs=[pl.BlockSpec(memory_space=pltpu.HBM)] * 9,
            out_specs=(vmem, vmem, vmem),
            scratch_shapes=list(scratch.values()),
            compiler_params=pltpu.CompilerParams(
                collective_id=0, has_side_effects=True, vmem_limit_bytes=16 << 20
            ),
            name="layer",
        )(
            *(
                pltpu.with_memory_space_constraint(v, pltpu.HBM)
                for v in (inputs, preact, cotangent, spectral_w, skip_w, *tables)
            )
        )
        outs = (gi, gs, gk.reshape(128, 128))

        def store(*refs):
            copies = [pltpu.make_async_copy(refs[n], refs[3 + n], refs[6].at[n]) for n in range(3)]
            for copy in copies:
                copy.start()
            for copy in copies:
                copy.wait()

        return pl.pallas_call(
            store,
            out_shape=tuple(jax.ShapeDtypeStruct(v.shape, v.dtype) for v in outs),
            in_specs=[any_space] * 3,
            out_specs=[pl.BlockSpec(memory_space=pltpu.HBM)] * 3,
            scratch_shapes=[pltpu.SemaphoreType.DMA((3,))],
            compiler_params=pltpu.CompilerParams(vmem_limit_bytes=4 << 20),
            name="store",
        )(*outs)

    cells = P("gx", "gy", None, None)
    weights = P("gx", "gy", None, None, None)
    return jax.shard_map(
        on_device,
        mesh=mesh,
        in_specs=(cells, cells, cells, weights, P()),
        out_specs=(cells, weights, P()),
        check_vma=False,
    )
```

```python
import functools
import math
from types import SimpleNamespace

import jax
import jax.numpy as jnp
import numpy as np
from jax import lax
from jax.experimental import pallas as pl
from jax.experimental.pallas import tpu as pltpu
from jax.sharding import PartitionSpec as P

MESH = pl.DeviceIdType.MESH
F32, BF16 = jnp.float32, jnp.bfloat16

NY, NX, NC = 4, 4, 2


def cas(modes, length):
    index = np.arange(modes)
    freq = np.where(index < modes // 2, index, length - modes + index)
    phase = freq[:, None] * np.arange(length)[None, :] % length
    angle = phase * (2.0 * math.pi / length)
    return (np.cos(angle) + np.sin(angle)) / math.sqrt(length)


def make_tables(s):
    fx = cas(2 * s.gx, 8 * s.gx)
    fy = cas(s.gy, 4 * s.gy)
    e = np.arange(2)
    jj, ii = np.arange(4), np.arange(8)
    cy, cx, cc, cj, ci = np.meshgrid(
        np.arange(NY), np.arange(NX), np.arange(NC), jj, ii, indexing="ij"
    )
    cy, cx, cc, cj, ci = (v.reshape(-1) for v in (cy, cx, cc, cj, ci))
    xt = np.zeros((s.zl, NY, s.zl, 2, s.cells))
    for zl in range(s.zl):
        cell_i = 8 * (s.zl * cy + zl) + ci
        for y in range(NY):
            for zd in range(s.zl):
                xt[zl, y, zd] = fx[2 * (s.zl * y + zd) + e][:, cell_i]
    yt = np.zeros((s.zh, s.zh, 2 * NX * NC, s.cells))
    xs, cs = (v.reshape(-1) for v in np.meshgrid(np.arange(NX), np.arange(NC), indexing="ij"))
    for zh in range(s.zh):
        cell_j = 4 * ((s.zh * cx + zh) * NC + cc) + cj
        for zd in range(s.zh):
            b = (xs * s.zh + zd) * NC + cs
            yt[zh, zd] = np.repeat(fy[b][:, cell_j], 2, axis=0)
    mh, ml, mx, mc, me = (
        v.reshape(-1)
        for v in np.meshgrid(
            np.arange(s.zh), np.arange(s.zl), np.arange(NX), np.arange(NC), e, indexing="ij"
        )
    )
    at = np.zeros((s.zl, NY, NY, 8, mh.size))
    for zl in range(s.zl):
        for q in range(NY):
            a = 2 * (s.zl * q + ml) + me
            for y in range(NY):
                at[zl, q, y] = fx[a][:, 8 * (s.zl * y + zl) + ii].T
    bt = np.zeros((s.zh, NX * NC, 4, mh.size))
    b = (mx * s.zh + mh) * NC + mc
    for zh in range(s.zh):
        for k in range(NX * NC):
            bt[zh, k] = fy[b][:, 4 * ((xs[k] * s.zh + zh) * NC + cs[k]) + jj].T
    return [jnp.asarray(v, F32) for v in (xt, yt, at, bt)]


def split(v):
    high = v.astype(BF16)
    return high, (v - high.astype(F32)).astype(BF16)


def kernel(s, inp, pre, cot, w, skw, xt, yt, at, bt, gi, gs, gk, r):
    gx, gy = lax.axis_index("gx"), lax.axis_index("gy")
    y, zl = gx // s.zl, gx % s.zl
    c, zh, x = gy % NC, (gy // NC) % s.zh, gy // (NC * s.zh)
    plane = (y * NX + x) * NC + c
    z = zh * s.zl + zl
    NP, NXC, NZ, NK = NY * NX * NC, NX * NC, s.zl * s.zh, s.nk

    def at_plane(dy, dx, dc):
        yy, xx, cc = (y + dy) % NY, (x + dx) % NX, (c + dc) % NC
        return yy, xx, cc, (yy * s.zl + zl, (xx * s.zh + zh) * NC + cc)

    def at_z(dz):
        zz = (z + dz) % NZ
        return zz, (y * s.zl + zz % s.zl, (x * s.zh + zz // s.zl) * NC + c)

    def hops(d, n):
        return min(d, n - d)

    plane_steps = sorted(
        (
            (dy, dx, dc)
            for dy in range(NY)
            for dx in range(NX)
            for dc in range(NC)
            if dy + dx + dc > 0
        ),
        key=lambda t: -(hops(t[0], NY) + hops(t[1], NX)),
    )
    z_steps = sorted(range(1, NZ), key=lambda d: -hops(d, NZ))

    def send(src, dst, name, device):
        pltpu.make_async_remote_copy(
            src_ref=src,
            dst_ref=dst,
            send_sem=r.send.at[s.phase[name]],
            recv_sem=r.recv.at[s.phase[name]],
            device_id=device,
            device_id_type=MESH,
        ).start()

    def wait(ref, count, name, sems):
        part = ref.at[pl.ds(0, count)]
        pltpu.make_async_copy(part, part, sems.at[s.phase[name]]).wait()

    reach = min(4, NZ // 2)
    near = [dz for dz in z_steps if hops(dz, NZ) <= reach]
    barrier = pltpu.get_barrier_semaphore()
    for step in plane_steps:
        pl.semaphore_signal(barrier, inc=1, device_id=at_plane(*step)[3], device_id_type=MESH)
    for dz in near:
        pl.semaphore_signal(barrier, inc=1, device_id=at_z(dz)[1], device_id_type=MESH)

    loads = [
        pltpu.make_async_copy(src, dst, r.local.at[n])
        for n, (src, dst) in enumerate(
            (
                (pre, r.pre),
                (cot, r.cot),
                (inp, r.inp),
                (skw, r.skw),
                (xt.at[zl, y], r.xt),
                (yt.at[zh], r.yt),
                (at.at[zl, y], r.at),
                (bt.at[zh], r.bt),
                (w, r.w),
            )
        )
    ]
    for copy in loads:
        copy.start()

    for n in range(2):
        loads[n].wait()
    rows = 32 * NK
    p = r.pre[...].astype(F32).reshape(rows, 128)
    slope = 0.5 * (1.0 + lax.erf(p * (1.0 / math.sqrt(2.0)))) + p * jnp.exp(-0.5 * p * p) * (
        1.0 / math.sqrt(2.0 * math.pi)
    )
    grad = (r.cot[...].astype(F32).reshape(rows, 128) * slope).astype(BF16)
    r.grad[...] = grad
    r.fields[1] = grad.astype(F32)

    def make_blocks(f):
        for k in range(NK):
            for j in range(0, 4, 2):
                pair = [
                    r.fields[f, pl.ds((j + o) * NK + k, 8, stride=4 * NK), :] for o in range(2)
                ]
                r.blocks[f, k, pl.ds(j * 8, 16), :] = jnp.concatenate(pair, axis=0).astype(BF16)

    make_blocks(1)

    pl.semaphore_wait(barrier, len(plane_steps) + len(near))
    relays = [dz for dz in near if hops(dz, NZ) == reach] if reach < NZ // 2 else []
    for dz in relays:
        pl.semaphore_signal(r.far, inc=1, device_id=at_z(dz)[1], device_id_type=MESH)

    xc = x * NC + c
    slot = z * NXC + xc

    def phase_a(f):
        for step in plane_steps:
            _, xx, cc, device = at_plane(*step)
            send(r.blocks.at[f, xx * NC + cc], r.slab.at[f, plane], f"A{f}", device)
        r.slab[f, plane] = r.blocks[f, xc]

    phase_a(1)

    order = z_steps + [0]
    loads[4].wait()
    loads[5].wait()
    for n, dz in enumerate(order):
        zd = (z + dz) % NZ
        yv = r.yt[zd // s.zl]
        xv = r.xt[zd % s.zl]
        high, low = split(jnp.concatenate([xv] * NXC, axis=0) * yv)
        r.th[n] = high
        r.tl[n] = low

    loads[2].wait()
    r.fields[0] = r.inp[...].astype(F32).reshape(rows, 128)
    make_blocks(0)
    local = lax.dot_general(
        r.fields[0].astype(BF16),
        r.grad[...],
        (((0,), (0,)), ((), ())),
        preferred_element_type=F32,
    )
    rk = 128 // NP
    for n in range(NP):
        r.skip_a[n] = local[n * rk : (n + 1) * rk]

    def sheet(dzs):
        steps = [(dz, dx, dc) for dz in dzs for dx in range(NX) for dc in range(NC)]
        return sorted(
            (t for t in steps if sum(t)), key=lambda t: -(hops(t[0], NZ) + hops(t[1], NX))
        )

    def at_sheet(dz, dx, dc):
        zz, xx, cc = (z + dz) % NZ, (x + dx) % NX, (c + dc) % NC
        return xx * NC + cc, (y * s.zl + zz % s.zl, (xx * s.zh + zz // s.zl) * NC + cc)

    def phase_b(f, chunks):
        slab = r.slab[f].reshape(s.cells, 128)
        chunk = NZ // chunks
        nm = chunk * 2 * NXC
        for g in range(0, NZ, chunk):
            parts = jnp.dot(
                r.th[g : g + chunk].reshape(nm, s.cells), slab, preferred_element_type=F32
            ) + jnp.dot(r.tl[g : g + chunk].reshape(nm, s.cells), slab, preferred_element_type=F32)
            r.parts[f, g : g + chunk] = parts.astype(BF16).reshape(chunk, NXC, 2, 128)
            for step in sheet(order[g : g + chunk]):
                k, device = at_sheet(*step)
                send(r.parts.at[f, order.index(step[0]), k], r.sums.at[f, slot], f"B{f}", device)
        r.sums[f, slot] = r.parts[f, NZ - 1, xc]

    row_steps = [t for t in plane_steps if t[0] == 0]
    if relays:
        pl.semaphore_wait(r.far, len(relays))
    for step in row_steps:
        pl.semaphore_signal(r.row, inc=1, device_id=at_plane(*step)[3], device_id_type=MESH)
    wait(r.slab.at[1], NP - 1, "A1", r.recv)
    pl.semaphore_wait(r.row, len(row_steps))
    phase_b(1, s.chunks)

    for step in plane_steps:
        yy, xx, cc, device = at_plane(*step)
        send(r.skip_a.at[(yy * NX + xx) * NC + cc], r.skip_b.at[plane], "SA", device)
    r.skip_b[plane] = r.skip_a[plane]
    loads[3].wait()
    r.skip[...] = lax.dot_general(
        r.grad[...], r.skw[...], (((1,), (1,)), ((), ())), preferred_element_type=F32
    )
    loads[6].wait()
    loads[7].wait()
    yorder = sorted(range(NY), key=lambda d: -hops(d, NY))

    @pl.loop(0, NP)
    def _(n):
        step = n // NXC
        dy = sum((jnp.where(step == g, d, 0) for g, d in enumerate(yorder)), 0)
        av = r.at[(y + dy) % NY]
        bv = r.bt[n % NXC]
        for j in range(0, 4, 2):
            high, low = split(
                jnp.concatenate([av * bv[j + o : j + o + 1] for o in range(2)], axis=0)
            )
            r.uh[n, pl.ds(j * 8, 16), :] = high
            r.ul[n, pl.ds(j * 8, 16), :] = low

    wait(r.skip_b, NP - 1, "SA", r.recv)
    phase_a(0)
    r.skip_c[...] = jnp.sum(r.skip_b[...], axis=0)
    for dz in z_steps:
        device = at_z(dz)[1]
        send(r.skip_c, r.skip_d.at[z], "SB", device)
    r.skip_d[z] = r.skip_c[...]

    def owned(f):
        wait(r.sums.at[f], NZ * NXC - 1, f"B{f}", r.recv)
        total = jnp.sum(r.sums[f].reshape(NZ, 2 * NXC, 128).astype(F32), axis=0)
        r.own[...] = total
        vals = [r.own[2 * k : 2 * k + 2] for k in range(NK)]
        for m in range(NK):
            total = vals[0] * s.fz[m][0]
            for k in range(1, NK):
                total += vals[k] * s.fz[m][k]
            r.modes[f, 2 * m : 2 * m + 2, :] = total

    loads[8].wait()
    owned(1)
    gm = r.modes[1]
    high, low = split(gm)
    lhs = jnp.concatenate([high, low], axis=0)
    nr = 2 * NK
    for m in range(NK):
        for e in range(2):
            d = lax.dot_general(
                lhs, r.w[e, 0, m], (((1,), (1,)), ((), ())), preferred_element_type=F32
            )
            row = 2 * m + e
            back = d[row : row + 1] + d[nr + row : nr + row + 1]
            r.back[row : row + 1, :] = back
    r.back_a[...] = r.back[...].astype(BF16).reshape(NK, 2, 128)

    for step in sheet(order):
        k, device = at_sheet(*step)
        send(r.back_a.at[k], r.gather.at[slot], "D", device)
    r.gather[slot] = r.back_a[xc]

    wait(r.slab.at[0], NP - 1, "A0", r.recv)
    phase_b(0, 1)

    wait(r.skip_d, NZ - 1, "SB", r.recv)
    r.skip_e[...] = jnp.sum(r.skip_d[...], axis=0) * s.scale
    for step in plane_steps:
        device = at_plane(*step)[3]
        send(r.skip_e, r.skip_f.at[plane], "SC", device)
    r.skip_f[plane] = r.skip_e[...]

    wait(r.gather, NZ * NXC - 1, "D", r.recv)
    gathered = r.gather[...].reshape(NZ * 2 * NXC, 128)
    nc = NXC * 32
    for g, dy in enumerate(yorder):
        part = slice(g * NXC, (g + 1) * NXC)
        cells = jnp.dot(
            r.uh[part].reshape(nc, NZ * 2 * NXC), gathered, preferred_element_type=F32
        ) + jnp.dot(r.ul[part].reshape(nc, NZ * 2 * NXC), gathered, preferred_element_type=F32)
        r.cells_a[part] = cells.astype(BF16).reshape(NXC, 32, 128)
        for step in plane_steps:
            if step[0] == dy:
                _, xx, cc, device = at_plane(*step)
                send(r.cells_a.at[g * NXC + xx * NC + cc], r.cells_b.at[plane], "F", device)
    r.cells_b[plane] = r.cells_a[yorder.index(0) * NXC + xc]

    owned(0)
    im = jnp.transpose(r.modes[0], (1, 0))
    for row in range(nr):
        gs[row % 2, 0, row // 2] = (im[:, row : row + 1] * gm[row : row + 1]).astype(BF16)

    wait(r.skip_f, NP - 1, "SC", r.recv)
    gk[...] = r.skip_f[...]

    wait(r.cells_b, NP - 1, "F", r.recv)
    vals = []
    for m in range(NK):
        total = r.cells_b[m].astype(F32)
        for q in range(1, NY):
            total += r.cells_b[q * NXC + m].astype(F32)
        vals.append(total)
    for k in range(NK):
        total = vals[0] * s.fz[0][k]
        for m in range(1, NK):
            total += vals[m] * s.fz[m][k]
        for j in range(4):
            r.fields[0, pl.ds(j * NK + k, 8, stride=4 * NK), :] = total[j * 8 : j * 8 + 8]
    gi[...] = (r.fields[0] + r.skip[...]).astype(BF16).reshape(gi.shape)

    for ref, count, name in (
        (r.slab.at[1], NP - 1, "A1"),
        (r.slab.at[0], NP - 1, "A0"),
        (r.skip_a, NP - 1, "SA"),
        (r.sums.at[1], NZ * NXC - 1, "B1"),
        (r.sums.at[0], NZ * NXC - 1, "B0"),
        (r.skip_d, NZ - 1, "SB"),
        (r.gather, NZ * NXC - 1, "D"),
        (r.skip_f, NP - 1, "SC"),
        (r.cells_b, NP - 1, "F"),
    ):
        wait(ref, count, name, r.send)


def solution(mesh):
    def on_device(inputs, preact, cotangent, spectral_w, skip_w):
        nk = inputs.shape[2]
        gx, gy = mesh.shape["gx"], mesh.shape["gy"]
        zl, zh = gx // NY, gy // (NX * NC)
        nz, np_, nxc = zl * zh, NY * NX * NC, NX * NC
        names = ("A0", "A1", "SA", "B0", "B1", "SB", "D", "SC", "F")
        table = cas(nk, nk)
        s = SimpleNamespace(
            gx=gx,
            gy=gy,
            zl=zl,
            zh=zh,
            nk=nk,
            cells=np_ * 32,
            chunks=2,
            fz=[[float(v) for v in row] for row in table],
            scale=1.0 / math.sqrt(gx * 8 * gy * 4 * nk),
            phase={name: n for n, name in enumerate(names)},
        )
        tables = make_tables(s)
        rk = 128 // np_
        V = pltpu.VMEM
        scratch = dict(
            inp=V(inputs.shape, BF16),
            pre=V(inputs.shape, BF16),
            cot=V(inputs.shape, BF16),
            skw=V((128, 128), BF16),
            w=V(spectral_w.shape, BF16),
            xt=V(tables[0].shape[2:], F32),
            yt=V(tables[1].shape[1:], F32),
            at=V(tables[2].shape[2:], F32),
            bt=V(tables[3].shape[1:], F32),
            fields=V((2, 32 * nk, 128), F32),
            grad=V((32 * nk, 128), BF16),
            skip=V((32 * nk, 128), F32),
            blocks=V((2, nk, 32, 128), BF16),
            slab=V((2, np_, 32, 128), BF16),
            th=V((nz, 2 * nxc, s.cells), BF16),
            tl=V((nz, 2 * nxc, s.cells), BF16),
            parts=V((2, nz, nxc, 2, 128), BF16),
            sums=V((2, nz * nxc, 2, 128), BF16),
            own=V((2 * nxc, 128), F32),
            modes=V((2, 2 * nk, 128), F32),
            back=V((2 * nk, 128), F32),
            back_a=V((nk, 2, 128), BF16),
            gather=V((nz * nxc, 2, 128), BF16),
            uh=V((np_, 32, nz * 2 * nxc), BF16),
            ul=V((np_, 32, nz * 2 * nxc), BF16),
            cells_a=V((np_, 32, 128), BF16),
            cells_b=V((np_, 32, 128), BF16),
            skip_a=V((np_, rk, 128), F32),
            skip_b=V((np_, rk, 128), F32),
            skip_c=V((rk, 128), F32),
            skip_d=V((nz, rk, 128), F32),
            skip_e=V((rk, 128), F32),
            skip_f=V((np_, rk, 128), F32),
            send=pltpu.SemaphoreType.DMA((len(names),)),
            recv=pltpu.SemaphoreType.DMA((len(names),)),
            local=pltpu.SemaphoreType.DMA((9,)),
            far=pltpu.SemaphoreType.REGULAR,
            row=pltpu.SemaphoreType.REGULAR,
        )

        def body(*refs):
            kernel(s, *refs[:12], SimpleNamespace(**dict(zip(scratch, refs[12:]))))

        any_space = pl.BlockSpec(memory_space=pl.ANY)
        vmem = pl.BlockSpec(memory_space=pltpu.VMEM)
        gi, gs, gk = pl.pallas_call(
            body,
            out_shape=(
                jax.ShapeDtypeStruct(inputs.shape, BF16),
                jax.ShapeDtypeStruct(spectral_w.shape, BF16),
                jax.ShapeDtypeStruct((np_, rk, 128), F32),
            ),
            in_specs=[pl.BlockSpec(memory_space=pltpu.HBM)] * 9,
            out_specs=(vmem, vmem, vmem),
            scratch_shapes=list(scratch.values()),
            compiler_params=pltpu.CompilerParams(
                collective_id=0, has_side_effects=True, vmem_limit_bytes=16 << 20
            ),
            name="layer",
        )(
            *(
                pltpu.with_memory_space_constraint(v, pltpu.HBM)
                for v in (inputs, preact, cotangent, spectral_w, skip_w, *tables)
            )
        )
        outs = (gi, gs, gk.reshape(128, 128))

        def store(*refs):
            copies = [pltpu.make_async_copy(refs[n], refs[3 + n], refs[6].at[n]) for n in range(3)]
            for copy in copies:
                copy.start()
            for copy in copies:
                copy.wait()

        return pl.pallas_call(
            store,
            out_shape=tuple(jax.ShapeDtypeStruct(v.shape, v.dtype) for v in outs),
            in_specs=[any_space] * 3,
            out_specs=[pl.BlockSpec(memory_space=pltpu.HBM)] * 3,
            scratch_shapes=[pltpu.SemaphoreType.DMA((3,))],
            compiler_params=pltpu.CompilerParams(vmem_limit_bytes=4 << 20),
            name="store",
        )(*outs)

    cells = P("gx", "gy", None, None)
    weights = P("gx", "gy", None, None, None)
    return jax.shard_map(
        on_device,
        mesh=mesh,
        in_specs=(cells, cells, cells, weights, P()),
        out_specs=(cells, weights, P()),
        check_vma=False,
    )
```

```python
import functools
import math
from types import SimpleNamespace

import jax
import jax.numpy as jnp
import numpy as np
from jax import lax
from jax.experimental import pallas as pl
from jax.experimental.pallas import tpu as pltpu
from jax.sharding import PartitionSpec as P

MESH = pl.DeviceIdType.MESH
F32, BF16 = jnp.float32, jnp.bfloat16

NY, NX, NC = 4, 4, 2


def cas(modes, length):
    index = np.arange(modes)
    freq = np.where(index < modes // 2, index, length - modes + index)
    phase = freq[:, None] * np.arange(length)[None, :] % length
    angle = phase * (2.0 * math.pi / length)
    return (np.cos(angle) + np.sin(angle)) / math.sqrt(length)


def make_tables(s):
    fx = cas(2 * s.gx, 8 * s.gx)
    fy = cas(s.gy, 4 * s.gy)
    e = np.arange(2)
    jj, ii = np.arange(4), np.arange(8)
    cy, cx, cc, cj, ci = np.meshgrid(
        np.arange(NY), np.arange(NX), np.arange(NC), jj, ii, indexing="ij"
    )
    cy, cx, cc, cj, ci = (v.reshape(-1) for v in (cy, cx, cc, cj, ci))
    xt = np.zeros((s.zl, NY, s.zl, 2, s.cells))
    for zl in range(s.zl):
        cell_i = 8 * (s.zl * cy + zl) + ci
        for y in range(NY):
            for zd in range(s.zl):
                xt[zl, y, zd] = fx[2 * (s.zl * y + zd) + e][:, cell_i]
    yt = np.zeros((s.zh, s.zh, 2 * NX * NC, s.cells))
    xs, cs = (v.reshape(-1) for v in np.meshgrid(np.arange(NX), np.arange(NC), indexing="ij"))
    for zh in range(s.zh):
        cell_j = 4 * ((s.zh * cx + zh) * NC + cc) + cj
        for zd in range(s.zh):
            b = (xs * s.zh + zd) * NC + cs
            yt[zh, zd] = np.repeat(fy[b][:, cell_j], 2, axis=0)
    mh, ml, mx, mc, me = (
        v.reshape(-1)
        for v in np.meshgrid(
            np.arange(s.zh), np.arange(s.zl), np.arange(NX), np.arange(NC), e, indexing="ij"
        )
    )
    at = np.zeros((s.zl, NY, NY, 8, mh.size))
    for zl in range(s.zl):
        for q in range(NY):
            a = 2 * (s.zl * q + ml) + me
            for y in range(NY):
                at[zl, q, y] = fx[a][:, 8 * (s.zl * y + zl) + ii].T
    bt = np.zeros((s.zh, NX * NC, 4, mh.size))
    b = (mx * s.zh + mh) * NC + mc
    for zh in range(s.zh):
        for k in range(NX * NC):
            bt[zh, k] = fy[b][:, 4 * ((xs[k] * s.zh + zh) * NC + cs[k]) + jj].T
    return [jnp.asarray(v, F32) for v in (xt, yt, at, bt)]


def split(v):
    high = v.astype(BF16)
    return high, (v - high.astype(F32)).astype(BF16)


def kernel(s, inp, pre, cot, w, skw, xt, yt, at, bt, gi, gs, gk, r):
    gx, gy = lax.axis_index("gx"), lax.axis_index("gy")
    y, zl = gx // s.zl, gx % s.zl
    c, zh, x = gy % NC, (gy // NC) % s.zh, gy // (NC * s.zh)
    plane = (y * NX + x) * NC + c
    z = zh * s.zl + zl
    NP, NXC, NZ, NK = NY * NX * NC, NX * NC, s.zl * s.zh, s.nk

    def at_plane(dy, dx, dc):
        yy, xx, cc = (y + dy) % NY, (x + dx) % NX, (c + dc) % NC
        return yy, xx, cc, (yy * s.zl + zl, (xx * s.zh + zh) * NC + cc)

    def at_z(dz):
        zz = (z + dz) % NZ
        return zz, (y * s.zl + zz % s.zl, (x * s.zh + zz // s.zl) * NC + c)

    def hops(d, n):
        return min(d, n - d)

    plane_steps = sorted(
        (
            (dy, dx, dc)
            for dy in range(NY)
            for dx in range(NX)
            for dc in range(NC)
            if dy + dx + dc > 0
        ),
        key=lambda t: -(hops(t[0], NY) + hops(t[1], NX)),
    )
    z_steps = sorted(range(1, NZ), key=lambda d: -hops(d, NZ))

    def send(src, dst, name, device):
        pltpu.make_async_remote_copy(
            src_ref=src,
            dst_ref=dst,
            send_sem=r.send.at[s.phase[name]],
            recv_sem=r.recv.at[s.phase[name]],
            device_id=device,
            device_id_type=MESH,
        ).start()

    def wait(ref, count, name, sems):
        part = ref.at[pl.ds(0, count)]
        pltpu.make_async_copy(part, part, sems.at[s.phase[name]]).wait()

    reach = min(4, NZ // 2)
    near = [dz for dz in z_steps if hops(dz, NZ) <= reach]
    barrier = pltpu.get_barrier_semaphore()
    for step in plane_steps:
        pl.semaphore_signal(barrier, inc=1, device_id=at_plane(*step)[3], device_id_type=MESH)
    for dz in near:
        pl.semaphore_signal(barrier, inc=1, device_id=at_z(dz)[1], device_id_type=MESH)

    loads = [
        pltpu.make_async_copy(src, dst, r.local.at[n])
        for n, (src, dst) in enumerate(
            (
                (pre, r.pre),
                (cot, r.cot),
                (inp, r.inp),
                (skw, r.skw),
                (xt.at[zl, y], r.xt),
                (yt.at[zh], r.yt),
                (at.at[zl, y], r.at),
                (bt.at[zh], r.bt),
                (w, r.w),
            )
        )
    ]
    for copy in loads:
        copy.start()

    for n in range(2):
        loads[n].wait()
    rows = 32 * NK
    p = r.pre[...].astype(F32).reshape(rows, 128)
    slope = 0.5 * (1.0 + lax.erf(p * (1.0 / math.sqrt(2.0)))) + p * jnp.exp(-0.5 * p * p) * (
        1.0 / math.sqrt(2.0 * math.pi)
    )
    grad = (r.cot[...].astype(F32).reshape(rows, 128) * slope).astype(BF16)
    r.grad[...] = grad
    r.fields[1] = grad.astype(F32)

    def make_blocks(f):
        for k in range(NK):
            for j in range(0, 4, 2):
                pair = [
                    r.fields[f, pl.ds((j + o) * NK + k, 8, stride=4 * NK), :] for o in range(2)
                ]
                r.blocks[f, k, pl.ds(j * 8, 16), :] = jnp.concatenate(pair, axis=0).astype(BF16)

    make_blocks(1)

    pl.semaphore_wait(barrier, len(plane_steps) + len(near))
    relays = [dz for dz in near if hops(dz, NZ) == reach] if reach < NZ // 2 else []
    for dz in relays:
        pl.semaphore_signal(r.far, inc=1, device_id=at_z(dz)[1], device_id_type=MESH)

    xc = x * NC + c
    slot = z * NXC + xc

    def phase_a(f):
        for step in plane_steps:
            _, xx, cc, device = at_plane(*step)
            send(r.blocks.at[f, xx * NC + cc], r.slab.at[f, plane], f"A{f}", device)
        r.slab[f, plane] = r.blocks[f, xc]

    phase_a(1)

    order = z_steps + [0]
    loads[4].wait()
    loads[5].wait()
    for n, dz in enumerate(order):
        zd = (z + dz) % NZ
        yv = r.yt[zd // s.zl]
        xv = r.xt[zd % s.zl]
        high, low = split(jnp.concatenate([xv] * NXC, axis=0) * yv)
        r.th[n] = high
        r.tl[n] = low

    loads[2].wait()
    r.fields[0] = r.inp[...].astype(F32).reshape(rows, 128)
    make_blocks(0)
    local = lax.dot_general(
        r.fields[0].astype(BF16),
        r.grad[...],
        (((0,), (0,)), ((), ())),
        preferred_element_type=F32,
    )
    rk = 128 // NP
    for n in range(NP):
        r.skip_a[n] = local[n * rk : (n + 1) * rk]

    def sheet(dzs):
        steps = [(dz, dx, dc) for dz in dzs for dx in range(NX) for dc in range(NC)]
        return sorted(
            (t for t in steps if sum(t)), key=lambda t: -(hops(t[0], NZ) + hops(t[1], NX))
        )

    def at_sheet(dz, dx, dc):
        zz, xx, cc = (z + dz) % NZ, (x + dx) % NX, (c + dc) % NC
        return xx * NC + cc, (y * s.zl + zz % s.zl, (xx * s.zh + zz // s.zl) * NC + cc)

    def phase_b(f, chunks):
        slab = r.slab[f].reshape(s.cells, 128)
        chunk = NZ // chunks
        nm = chunk * 2 * NXC
        for g in range(0, NZ, chunk):
            parts = jnp.dot(
                r.th[g : g + chunk].reshape(nm, s.cells), slab, preferred_element_type=F32
            ) + jnp.dot(r.tl[g : g + chunk].reshape(nm, s.cells), slab, preferred_element_type=F32)
            r.parts[f, g : g + chunk] = parts.astype(BF16).reshape(chunk, NXC, 2, 128)
            for step in sheet(order[g : g + chunk]):
                k, device = at_sheet(*step)
                send(r.parts.at[f, order.index(step[0]), k], r.sums.at[f, slot], f"B{f}", device)
        r.sums[f, slot] = r.parts[f, NZ - 1, xc]

    row_steps = [t for t in plane_steps if t[0] == 0]
    if relays:
        pl.semaphore_wait(r.far, len(relays))
    for step in row_steps:
        pl.semaphore_signal(r.row, inc=1, device_id=at_plane(*step)[3], device_id_type=MESH)
    wait(r.slab.at[1], NP - 1, "A1", r.recv)
    pl.semaphore_wait(r.row, len(row_steps))
    phase_b(1, s.chunks)

    for step in plane_steps:
        yy, xx, cc, device = at_plane(*step)
        send(r.skip_a.at[(yy * NX + xx) * NC + cc], r.skip_b.at[plane], "SA", device)
    r.skip_b[plane] = r.skip_a[plane]
    loads[3].wait()
    r.skip[...] = lax.dot_general(
        r.grad[...], r.skw[...], (((1,), (1,)), ((), ())), preferred_element_type=F32
    )
    loads[6].wait()
    loads[7].wait()
    yorder = sorted(range(NY), key=lambda d: -hops(d, NY))

    @pl.loop(0, NP)
    def _(n):
        step = n // NXC
        dy = sum((jnp.where(step == g, d, 0) for g, d in enumerate(yorder)), 0)
        av = r.at[(y + dy) % NY]
        bv = r.bt[n % NXC]
        for j in range(0, 4, 2):
            high, low = split(
                jnp.concatenate([av * bv[j + o : j + o + 1] for o in range(2)], axis=0)
            )
            r.uh[n, pl.ds(j * 8, 16), :] = high
            r.ul[n, pl.ds(j * 8, 16), :] = low

    wait(r.skip_b, NP - 1, "SA", r.recv)
    phase_a(0)
    r.skip_c[...] = jnp.sum(r.skip_b[...], axis=0)
    for dz in z_steps:
        device = at_z(dz)[1]
        send(r.skip_c, r.skip_d.at[z], "SB", device)
    r.skip_d[z] = r.skip_c[...]

    def owned(f):
        wait(r.sums.at[f], NZ * NXC - 1, f"B{f}", r.recv)
        total = jnp.sum(r.sums[f].reshape(NZ, 2 * NXC, 128).astype(F32), axis=0)
        r.own[...] = total
        vals = [r.own[2 * k : 2 * k + 2] for k in range(NK)]
        for m in range(NK):
            total = vals[0] * s.fz[m][0]
            for k in range(1, NK):
                total += vals[k] * s.fz[m][k]
            r.modes[f, 2 * m : 2 * m + 2, :] = total

    loads[8].wait()
    owned(1)
    gm = r.modes[1]
    high, low = split(gm)
    lhs = jnp.concatenate([high, low], axis=0)
    nr = 2 * NK
    for m in range(NK):
        for e in range(2):
            d = lax.dot_general(
                lhs, r.w[e, 0, m], (((1,), (1,)), ((), ())), preferred_element_type=F32
            )
            row = 2 * m + e
            back = d[row : row + 1] + d[nr + row : nr + row + 1]
            r.back[row : row + 1, :] = back
    r.back_a[...] = r.back[...].astype(BF16).reshape(NK, 2, 128)

    for step in sheet(order):
        k, device = at_sheet(*step)
        send(r.back_a.at[k], r.gather.at[slot], "D", device)
    r.gather[slot] = r.back_a[xc]

    wait(r.skip_d, NZ - 1, "SB", r.recv)
    r.skip_e[...] = jnp.sum(r.skip_d[...], axis=0) * s.scale
    for step in plane_steps:
        device = at_plane(*step)[3]
        send(r.skip_e, r.skip_f.at[plane], "SC", device)
    r.skip_f[plane] = r.skip_e[...]

    wait(r.slab.at[0], NP - 1, "A0", r.recv)
    phase_b(0, 1)

    wait(r.gather, NZ * NXC - 1, "D", r.recv)
    gathered = r.gather[...].reshape(NZ * 2 * NXC, 128)
    nc = NXC * 32
    for g, dy in enumerate(yorder):
        part = slice(g * NXC, (g + 1) * NXC)
        cells = jnp.dot(
            r.uh[part].reshape(nc, NZ * 2 * NXC), gathered, preferred_element_type=F32
        ) + jnp.dot(r.ul[part].reshape(nc, NZ * 2 * NXC), gathered, preferred_element_type=F32)
        r.cells_a[part] = cells.astype(BF16).reshape(NXC, 32, 128)
        for step in plane_steps:
            if step[0] == dy:
                _, xx, cc, device = at_plane(*step)
                send(r.cells_a.at[g * NXC + xx * NC + cc], r.cells_b.at[plane], "F", device)
    r.cells_b[plane] = r.cells_a[yorder.index(0) * NXC + xc]

    owned(0)
    im = jnp.transpose(r.modes[0], (1, 0))
    for row in range(nr):
        gs[row % 2, 0, row // 2] = (im[:, row : row + 1] * gm[row : row + 1]).astype(BF16)

    wait(r.skip_f, NP - 1, "SC", r.recv)
    gk[...] = r.skip_f[...]

    wait(r.cells_b, NP - 1, "F", r.recv)
    vals = []
    for m in range(NK):
        total = r.cells_b[m].astype(F32)
        for q in range(1, NY):
            total += r.cells_b[q * NXC + m].astype(F32)
        vals.append(total)
    for k in range(NK):
        total = vals[0] * s.fz[0][k]
        for m in range(1, NK):
            total += vals[m] * s.fz[m][k]
        for j in range(4):
            r.fields[0, pl.ds(j * NK + k, 8, stride=4 * NK), :] = total[j * 8 : j * 8 + 8]
    gi[...] = (r.fields[0] + r.skip[...]).astype(BF16).reshape(gi.shape)

    for ref, count, name in (
        (r.slab.at[1], NP - 1, "A1"),
        (r.slab.at[0], NP - 1, "A0"),
        (r.skip_a, NP - 1, "SA"),
        (r.sums.at[1], NZ * NXC - 1, "B1"),
        (r.sums.at[0], NZ * NXC - 1, "B0"),
        (r.skip_d, NZ - 1, "SB"),
        (r.gather, NZ * NXC - 1, "D"),
        (r.skip_f, NP - 1, "SC"),
        (r.cells_b, NP - 1, "F"),
    ):
        wait(ref, count, name, r.send)


def solution(mesh):
    def on_device(inputs, preact, cotangent, spectral_w, skip_w):
        nk = inputs.shape[2]
        gx, gy = mesh.shape["gx"], mesh.shape["gy"]
        zl, zh = gx // NY, gy // (NX * NC)
        nz, np_, nxc = zl * zh, NY * NX * NC, NX * NC
        names = ("A0", "A1", "SA", "B0", "B1", "SB", "D", "SC", "F")
        table = cas(nk, nk)
        s = SimpleNamespace(
            gx=gx,
            gy=gy,
            zl=zl,
            zh=zh,
            nk=nk,
            cells=np_ * 32,
            chunks=2,
            fz=[[float(v) for v in row] for row in table],
            scale=1.0 / math.sqrt(gx * 8 * gy * 4 * nk),
            phase={name: n for n, name in enumerate(names)},
        )
        tables = make_tables(s)
        rk = 128 // np_
        V = pltpu.VMEM
        scratch = dict(
            inp=V(inputs.shape, BF16),
            pre=V(inputs.shape, BF16),
            cot=V(inputs.shape, BF16),
            skw=V((128, 128), BF16),
            w=V(spectral_w.shape, BF16),
            xt=V(tables[0].shape[2:], F32),
            yt=V(tables[1].shape[1:], F32),
            at=V(tables[2].shape[2:], F32),
            bt=V(tables[3].shape[1:], F32),
            fields=V((2, 32 * nk, 128), F32),
            grad=V((32 * nk, 128), BF16),
            skip=V((32 * nk, 128), F32),
            blocks=V((2, nk, 32, 128), BF16),
            slab=V((2, np_, 32, 128), BF16),
            th=V((nz, 2 * nxc, s.cells), BF16),
            tl=V((nz, 2 * nxc, s.cells), BF16),
            parts=V((2, nz, nxc, 2, 128), BF16),
            sums=V((2, nz * nxc, 2, 128), BF16),
            own=V((2 * nxc, 128), F32),
            modes=V((2, 2 * nk, 128), F32),
            back=V((2 * nk, 128), F32),
            back_a=V((nk, 2, 128), BF16),
            gather=V((nz * nxc, 2, 128), BF16),
            uh=V((np_, 32, nz * 2 * nxc), BF16),
            ul=V((np_, 32, nz * 2 * nxc), BF16),
            cells_a=V((np_, 32, 128), BF16),
            cells_b=V((np_, 32, 128), BF16),
            skip_a=V((np_, rk, 128), F32),
            skip_b=V((np_, rk, 128), F32),
            skip_c=V((rk, 128), F32),
            skip_d=V((nz, rk, 128), F32),
            skip_e=V((rk, 128), F32),
            skip_f=V((np_, rk, 128), F32),
            send=pltpu.SemaphoreType.DMA((len(names),)),
            recv=pltpu.SemaphoreType.DMA((len(names),)),
            local=pltpu.SemaphoreType.DMA((9,)),
            far=pltpu.SemaphoreType.REGULAR,
            row=pltpu.SemaphoreType.REGULAR,
        )

        def body(*refs):
            kernel(s, *refs[:12], SimpleNamespace(**dict(zip(scratch, refs[12:]))))

        any_space = pl.BlockSpec(memory_space=pl.ANY)
        vmem = pl.BlockSpec(memory_space=pltpu.VMEM)
        gi, gs, gk = pl.pallas_call(
            body,
            out_shape=(
                jax.ShapeDtypeStruct(inputs.shape, BF16),
                jax.ShapeDtypeStruct(spectral_w.shape, BF16),
                jax.ShapeDtypeStruct((np_, rk, 128), F32),
            ),
            in_specs=[pl.BlockSpec(memory_space=pltpu.HBM)] * 9,
            out_specs=(vmem, vmem, vmem),
            scratch_shapes=list(scratch.values()),
            compiler_params=pltpu.CompilerParams(
                collective_id=0, has_side_effects=True, vmem_limit_bytes=16 << 20
            ),
            name="layer",
        )(
            *(
                pltpu.with_memory_space_constraint(v, pltpu.HBM)
                for v in (inputs, preact, cotangent, spectral_w, skip_w, *tables)
            )
        )
        outs = (gi, gs, gk.reshape(128, 128))

        def store(*refs):
            copies = [pltpu.make_async_copy(refs[n], refs[3 + n], refs[6].at[n]) for n in range(3)]
            for copy in copies:
                copy.start()
            for copy in copies:
                copy.wait()

        return pl.pallas_call(
            store,
            out_shape=tuple(jax.ShapeDtypeStruct(v.shape, v.dtype) for v in outs),
            in_specs=[any_space] * 3,
            out_specs=[pl.BlockSpec(memory_space=pltpu.HBM)] * 3,
            scratch_shapes=[pltpu.SemaphoreType.DMA((3,))],
            compiler_params=pltpu.CompilerParams(vmem_limit_bytes=4 << 20),
            name="store",
        )(*outs)

    cells = P("gx", "gy", None, None)
    weights = P("gx", "gy", None, None, None)
    return jax.shard_map(
        on_device,
        mesh=mesh,
        in_specs=(cells, cells, cells, weights, P()),
        out_specs=(cells, weights, P()),
        check_vma=False,
    )
```
